128 devices in a mesh: row: 8 (over z_lo, x), col: 16 (over y, z_hi, core).
Axes of the slice: x: 4, y: 4, z: 4 (z_hi: 2, z_lo: 2; z = z_hi * 2 + z_lo), core: 2. Of those that a mesh axis runs over, the one named last changes fastest.
Arguments:
- pair_act: bfloat16 [512, 512, 128], P('row', 'col'), may hold values from -6 to 6
- out_grad: bfloat16 [512, 512, 128], P('row', 'col'), may hold values from -6 to 6
- tri_bias: bfloat16 [4, 512, 512], P(None, 'row', 'col'), may hold values from -6 to 250
- w_query: bfloat16 [128, 128], replicated, may hold values from -0.5 to 0.5
- w_key: bfloat16 [128, 128], replicated, may hold values from -0.5 to 0.5
- w_value: bfloat16 [128, 128], replicated, may hold values from -0.5 to 0.5
- w_gate: bfloat16 [128, 128], replicated, may hold values from -0.5 to 0.5
- w_out: bfloat16 [128, 128], replicated, may hold values from -0.5 to 0.5
- key_blocks: int32 [4, 3], replicated, may hold values from 0 to 3, as said below
- list_len: int32 [4], replicated, may hold values from 1 to 3, as said below
Outputs:
- d_pair: bfloat16 [512, 512, 128], P('row', 'col')
- d_bias: float32 [4, 512, 512], P(None, 'row', 'col')
- d_w_query: float32 [128, 128], replicated
- d_w_key: float32 [128, 128], replicated
- d_w_value: float32 [128, 128], replicated
- d_w_gate: float32 [128, 128], replicated
- d_w_out: float32 [128, 128], replicated
The draws below stay inside these ranges and needn't reach their ends.
Inputs may be any that keep to these rules, and one draw needn't show every extreme that they name: `key_blocks`: entry 0 of query block b's list is b itself; its first list_len[b] entries are distinct; entries past list_len[b] are block numbers that must be ignored. `list_len`: some query block lists 3 key blocks.
All inputs are finite; a program needn't handle non-finite values.
Results may differ from the reference program's by a relative error of at most 0.015.
Values may be sent and summed in bfloat16 or wider, within the bound.
A program may use at most 128 MiB of HBM per device.

```python
import jax
import jax.numpy as jnp
from jax import lax

CHAN = 128
HEADS = 4
HEAD_DIM = 32
PROJ = 128
BLOCK = 128
QBLOCKS = 4
LISTED = 3
TOKENS = 512


def draw_tri_bias(key, part):
    base_key = jax.random.fold_in(jax.random.fold_in(key, 11), 0)
    full_shape = (HEADS, TOKENS, TOKENS)
    base = jnp.clip(jax.random.normal(base_key, full_shape, jnp.float32), -6.0, 6.0)
    return base.astype(jnp.bfloat16)


def list_tables(key):
    score_key, len_key, pick_key = jax.random.split(jax.random.fold_in(key, 29), 3)
    block_ids = jnp.arange(QBLOCKS, dtype=jnp.int32)
    ranking = jax.random.randint(score_key, (QBLOCKS, QBLOCKS), 0, 1048576) * QBLOCKS + block_ids[None, :]
    ranking = jnp.where(block_ids[:, None] == block_ids[None, :], -1, ranking)
    ordering = jnp.argsort(ranking, axis=1, stable=True)[:, :LISTED].astype(jnp.int32)
    lengths = jax.random.randint(len_key, (QBLOCKS,), 1, LISTED + 1)
    chosen_row = jax.random.randint(pick_key, (), 0, QBLOCKS)
    lengths = jnp.where(block_ids == chosen_row, LISTED, lengths).astype(jnp.int32)
    return (ordering, lengths)


def draw_key_blocks(key, part):
    return list_tables(key)[0]


def draw_list_len(key, part):
    return list_tables(key)[1]


def levels(rng, extent, cuts, low, high):
    def one(position, blocks):
        steps = jax.random.uniform(jax.random.fold_in(jax.random.fold_in(rng, 6), position), (blocks,), jnp.float32, low / len(cuts), high / len(cuts))
        return jnp.repeat(jnp.exp(steps), extent[position] // blocks).reshape((-1,) + (1,) * (len(extent) - position - 1))

    loudness = one(*cuts[0])
    for cut in cuts[1:]:
        loudness = loudness * one(*cut)
    return loudness


def noise(rng, shape, scale, most, cuts=(), kind=jnp.bfloat16):
    result = jax.random.normal(rng, shape, jnp.float32) * scale
    if len(cuts) > 0:
        result = levels(rng, shape, cuts, -0.22, 0.18) * result
    return jnp.clip(result, min=-most, max=most).astype(kind)


def setup_inputs(seed: int = 0) -> dict:
    key_list = jax.random.split(jax.random.key(seed), 11)
    return {
        "pair_act": noise(key_list[0], (TOKENS, TOKENS, CHAN), 1.0, 6.0, ((0, 8), (1, 16))),
        "out_grad": noise(key_list[1], (TOKENS, TOKENS, CHAN), 1.0, 6.0, ((0, 8), (1, 16))),
        "tri_bias": draw_tri_bias(jax.random.fold_in(key_list[10], 71), 0),
        "w_query": noise(key_list[3], (CHAN, PROJ), CHAN ** -0.5, 0.5),
        "w_key": noise(key_list[4], (CHAN, PROJ), CHAN ** -0.5, 0.5),
        "w_value": noise(key_list[5], (CHAN, PROJ), CHAN ** -0.5, 0.5),
        "w_gate": noise(key_list[6], (CHAN, PROJ), CHAN ** -0.5, 0.5),
        "w_out": noise(key_list[7], (PROJ, CHAN), PROJ ** -0.5, 0.5),
        "key_blocks": draw_key_blocks(jax.random.fold_in(key_list[10], 71), 0),
        "list_len": draw_list_len(jax.random.fold_in(key_list[10], 71), 0),
    }


def token_mask(key_blocks, list_len):
    block_count = key_blocks.shape[0]
    live_slots = jnp.arange(key_blocks.shape[1])[None, :] < list_len[:, None]
    block_hits = (key_blocks[:, :, None] == jnp.arange(block_count)[None, None, :]) & live_slots[:, :, None]
    block_allowed = jnp.any(block_hits, axis=1)
    return jnp.repeat(jnp.repeat(block_allowed, BLOCK, axis=0), BLOCK, axis=1)


def rounded(value):
    return lax.optimization_barrier(value.astype(jnp.bfloat16)).astype(jnp.float32)


def reference(pair_act, out_grad, tri_bias, w_query, w_key, w_value, w_gate, w_out, key_blocks, list_len):
    score_scale = HEAD_DIM ** -0.5
    allowed = token_mask(key_blocks, list_len)
    bias_t = jnp.transpose(tri_bias.astype(jnp.float32), (0, 2, 1))
    col_step = 4
    step_count = TOKENS // col_step
    col_acts = jnp.transpose(pair_act.reshape(TOKENS, step_count, col_step, CHAN), (1, 0, 2, 3))
    col_grads = jnp.transpose(out_grad.reshape(TOKENS, step_count, col_step, CHAN), (1, 0, 2, 3))
    head_shape = (TOKENS, col_step, HEADS, HEAD_DIM)

    def one_step(running, inputs):
        bias_acc, wq_acc, wk_acc, wv_acc, wg_acc, wo_acc = running
        act_block, grad_block = inputs
        flat_acts = act_block.reshape(-1, CHAN)
        flat_grads = grad_block.reshape(-1, CHAN)
        queries = (jnp.dot(flat_acts, w_query, preferred_element_type=jnp.float32) * score_scale).astype(jnp.bfloat16)
        key_proj = jnp.dot(flat_acts, w_key, preferred_element_type=jnp.float32).astype(jnp.bfloat16)
        values = jnp.dot(flat_acts, w_value, preferred_element_type=jnp.float32).astype(jnp.bfloat16)
        gate_act = jax.nn.sigmoid(jnp.dot(flat_acts, w_gate, preferred_element_type=jnp.float32))
        query_four = queries.reshape(head_shape).astype(jnp.float32)
        key_four = key_proj.reshape(head_shape).astype(jnp.float32)
        value_four = values.reshape(head_shape).astype(jnp.float32)
        scores = jnp.einsum('ichd,kchd->chik', query_four, key_four) + bias_t[None]
        scores = jnp.where(allowed[None, None], scores, -jnp.inf)
        row_peak = jnp.max(scores, axis=-1, keepdims=True)
        exp_scores = jnp.exp(scores - row_peak)
        att_probs = exp_scores / jnp.sum(exp_scores, axis=-1, keepdims=True)
        probs_low = rounded(att_probs)
        attended = jnp.einsum('chik,kchd->ichd', probs_low, value_four).reshape(-1, PROJ)
        gated = (gate_act * attended).astype(jnp.bfloat16)
        d_gated = lax.dot_general(flat_grads, w_out, (((1,), (1,)), ((), ())), preferred_element_type=jnp.float32)
        d_att = (d_gated * gate_act).astype(jnp.bfloat16)
        d_gpre = (d_gated * attended * gate_act * (1.0 - gate_act)).astype(jnp.bfloat16)
        att_four = d_att.reshape(head_shape).astype(jnp.float32)
        d_probs = jnp.einsum('ichd,kchd->chik', att_four, value_four)
        delta_sum = jnp.einsum('ichd,ichd->chi', att_four, attended.reshape(head_shape))[..., None]
        d_scores = att_probs * (d_probs - delta_sum)
        ds_low = rounded(d_scores)
        d_query = (jnp.einsum('chik,kchd->ichd', ds_low, key_four) * score_scale).reshape(-1, PROJ).astype(jnp.bfloat16)
        d_keys = jnp.einsum('chik,ichd->kchd', ds_low, query_four).reshape(-1, PROJ).astype(jnp.bfloat16)
        d_values = jnp.einsum('chik,ichd->kchd', probs_low, att_four).reshape(-1, PROJ).astype(jnp.bfloat16)
        d_flat = (jnp.dot(d_query, w_query.T, preferred_element_type=jnp.float32)
                  + jnp.dot(d_keys, w_key.T, preferred_element_type=jnp.float32)
                  + jnp.dot(d_values, w_value.T, preferred_element_type=jnp.float32)
                  + jnp.dot(d_gpre, w_gate.T, preferred_element_type=jnp.float32)).astype(jnp.bfloat16)
        acts_t = flat_acts.T
        running = (bias_acc + jnp.sum(d_scores, axis=0),
                   wq_acc + jnp.dot(acts_t, d_query, preferred_element_type=jnp.float32),
                   wk_acc + jnp.dot(acts_t, d_keys, preferred_element_type=jnp.float32),
                   wv_acc + jnp.dot(acts_t, d_values, preferred_element_type=jnp.float32),
                   wg_acc + jnp.dot(acts_t, d_gpre, preferred_element_type=jnp.float32),
                   wo_acc + jnp.dot(gated.T, flat_grads, preferred_element_type=jnp.float32))
        return running, d_flat.reshape(TOKENS, col_step, CHAN)

    start = (jnp.zeros((HEADS, TOKENS, TOKENS), jnp.float32),
             jnp.zeros((CHAN, PROJ), jnp.float32), jnp.zeros((CHAN, PROJ), jnp.float32),
             jnp.zeros((CHAN, PROJ), jnp.float32), jnp.zeros((CHAN, PROJ), jnp.float32),
             jnp.zeros((PROJ, CHAN), jnp.float32))
    final, pieces = lax.scan(one_step, start, (col_acts, col_grads))
    d_pair = jnp.transpose(pieces, (1, 0, 2, 3)).reshape(TOKENS, TOKENS, CHAN)
    d_bias = jnp.transpose(final[0], (0, 2, 1))
    return (d_pair, d_bias, final[1], final[2], final[3], final[4], final[5])
```

```python
import jax
import jax.numpy as jnp
from jax import lax
from jax.experimental import pallas as pl
from jax.experimental.pallas import tpu as pltpu
from jax.sharding import PartitionSpec as P

BF = jnp.bfloat16
F32 = jnp.float32
HEADS = 4
HEAD_DIM = 32
PROJ = HEADS * HEAD_DIM
BLOCK = 128
QBLOCKS = 4
SLOTS = 3
TOKENS = QBLOCKS * BLOCK
WIDE = SLOTS * BLOCK
ALL = HEADS * WIDE
ROWS = 8
COLS = 16
TILE_ROWS = TOKENS // ROWS
TILE_COLS = TOKENS // COLS
COL_WIDTH = TILE_COLS // ROWS
WROWS = 5 * PROJ
WPART = WROWS // ROWS
DEAD = -1e30
SCALE = HEAD_DIM ** -0.5

ROW_OFFS = [(dz, dx) for dz in range(2) for dx in range(4)][1:]
COL_OFFS = [(dy, dz, dc) for dy in range(4) for dz in range(2) for dc in range(2)][1:]


def row_peer(r, off):
    z, x = r // 4, lax.rem(r, 4)
    return lax.rem(z + off[0], 2) * 4 + lax.rem(x + off[1], 4)


def col_peer(c, off):
    y, z, k = c // 4, lax.rem(c // 2, 2), lax.rem(c, 2)
    return lax.rem(y + off[0], 4) * 4 + lax.rem(z + off[1], 2) * 2 + lax.rem(k + off[2], 2)


def remote(src, dst, ssem, rsem, r, c):
    return pltpu.make_async_remote_copy(
        src_ref=src,
        dst_ref=dst,
        send_sem=ssem,
        recv_sem=rsem,
        device_id=(r, c),
        device_id_type=pl.DeviceIdType.MESH,
    )


def greet(r, c, col_offs):
    sem = pltpu.get_barrier_semaphore()
    for off in ROW_OFFS:
        pl.semaphore_signal(
            sem, inc=1, device_id=(row_peer(r, off), c), device_id_type=pl.DeviceIdType.MESH
        )
    for off in col_offs:
        pl.semaphore_signal(
            sem, inc=1, device_id=(r, col_peer(c, off)), device_id_type=pl.DeviceIdType.MESH
        )
    pl.semaphore_wait(sem, len(ROW_OFFS) + len(col_offs))


IN_COLS = [(0, 0, 1), (0, 1, 0), (1, 0, 0), (2, 0, 0), (3, 0, 0)]


def in_kernel(
    kb_ref, len_ref, act_ref, grad_ref, bias_ref, acol_ref, gcol_ref, full_ref,
    got, turned, mine, sa, ra, sg, rg, sb, rb, sz, rz, sc, rc, sy, ry, sf, rf, sl,
):
    r, c = lax.axis_index("row"), lax.axis_index("col")
    y = c // 4
    greet(r, c, IN_COLS)
    first = []
    for n, off in enumerate(ROW_OFFS):
        p = row_peer(r, off)
        cp = remote(bias_ref, got.at[r], sb.at[n], rb.at[n], p, c)
        cp.start()
        first.append(cp)
    rows = pl.ds(r * TILE_ROWS, TILE_ROWS)
    big = []
    for n, off in enumerate(ROW_OFFS):
        p = row_peer(r, off)
        part = pl.ds(p * COL_WIDTH, COL_WIDTH)
        ca = remote(act_ref.at[part], acol_ref.at[:, rows, :], sa.at[n], ra.at[n], p, c)
        cg = remote(grad_ref.at[part], gcol_ref.at[:, rows, :], sg.at[n], rg.at[n], p, c)
        ca.start()
        cg.start()
        big += [ca, cg]
    own = pl.ds(r * COL_WIDTH, COL_WIDTH)
    la = pltpu.make_async_copy(act_ref.at[own], acol_ref.at[:, rows, :], sl.at[0])
    lg = pltpu.make_async_copy(grad_ref.at[own], gcol_ref.at[:, rows, :], sl.at[1])
    la.start()
    lg.start()
    got[r] = bias_ref[...]
    for cp in first:
        cp.wait()
    for k in range(QBLOCKS):
        pair = jnp.concatenate([got[2 * k], got[2 * k + 1]], axis=0).astype(F32)
        turned[k] = pair.T.astype(BF)
    for s in range(SLOTS):
        tile = turned[kb_ref[y, s]]
        tile = jnp.where(s < len_ref[y], tile.astype(F32), DEAD).astype(BF)
        for h in range(HEADS):
            mine[:, h * WIDE + s * BLOCK : h * WIDE + (s + 1) * BLOCK] = tile[
                h * HEAD_DIM : (h + 1) * HEAD_DIM, :
            ]

    def piece(cc):
        return full_ref.at[pl.ds(cc * TILE_COLS, TILE_COLS), :]

    sends = []
    zc = col_peer(c, (0, 1, 0))
    sib = col_peer(c, (0, 0, 1))
    cz = remote(mine, piece(c), sz.at[0], rz.at[0], r, zc)
    cz.start()
    to_y = []
    for n in range(3):
        cp = remote(mine, piece(c), sy.at[n], ry.at[n], r, col_peer(c, (n + 1, 0, 0)))
        cp.start()
        to_y.append(cp)
    cs = remote(mine, piece(c), sc.at[0], rc.at[0], r, sib)
    cs.start()
    lm = pltpu.make_async_copy(mine, piece(c), sl.at[2])
    lm.start()

    def forward(n, cc):
        cp = remote(piece(cc), piece(cc), sf.at[n], rf.at[n], r, sib)
        cp.start()
        sends.append(cp)

    cz.wait_recv()
    for n in range(3):
        cp = remote(piece(zc), piece(zc), sy.at[3 + n], ry.at[3 + n], r, col_peer(c, (n + 1, 0, 0)))
        cp.start()
        to_y.append(cp)
    forward(0, zc)
    for n in range(3):
        to_y[n].wait_recv()
        forward(1 + n, col_peer(c, (3 - n, 0, 0)))
    for n in range(3):
        to_y[3 + n].wait_recv()
        forward(4 + n, col_peer(c, (3 - n, 1, 0)))
    cz.wait_send()
    for cp in to_y:
        cp.wait_send()
    cs.wait()
    for cp in sends:
        cp.wait()
    for cp in big:
        cp.wait()
    la.wait()
    lg.wait()
    lm.wait()


def gather_in(key_blocks, list_len, act, grad, bias):
    any_ = pl.BlockSpec(memory_space=pl.ANY)
    smem = pl.BlockSpec(memory_space=pltpu.SMEM)
    vmem = pl.BlockSpec(memory_space=pltpu.VMEM)
    dma = pltpu.SemaphoreType.DMA
    return pl.pallas_call(
        in_kernel,
        out_shape=(
            jax.ShapeDtypeStruct((COL_WIDTH, TOKENS, PROJ), BF),
            jax.ShapeDtypeStruct((COL_WIDTH, TOKENS, PROJ), BF),
            jax.ShapeDtypeStruct((TOKENS, ALL), BF),
        ),
        in_specs=[smem, smem, any_, any_, vmem],
        out_specs=(any_, any_, any_),
        scratch_shapes=[
            pltpu.VMEM((ROWS, TILE_ROWS, PROJ), BF),
            pltpu.VMEM((QBLOCKS, PROJ, BLOCK), BF),
            pltpu.VMEM((TILE_COLS, ALL), BF),
            dma((7,)), dma((7,)), dma((7,)), dma((7,)), dma((7,)), dma((7,)),
            dma((1,)), dma((1,)), dma((1,)), dma((1,)), dma((6,)), dma((6,)), dma((7,)), dma((7,)),
            dma((3,)),
        ],
        compiler_params=pltpu.CompilerParams(collective_id=0, has_side_effects=True),
        name="gather_in",
    )(key_blocks, list_len, act, grad, bias)


NT = (((1,), (1,)), ((), ()))
NN = (((1,), (0,)), ((), ()))


def mm(a, b, dims=NN):
    return lax.dot_general(a, b, dims, preferred_element_type=F32)


def main_kernel(
    kb_ref, act_ref, grad_ref, bias_ref, w_ref, wo_ref, dpair_ref, dbias_ref, dw_ref,
    q_s, k_s, v_s, g_s, dg_s, dq_s, dgp_s, gated_s, dkt_s, dvt_s, dacc_s, dw_s, dwo_s,
):
    head_of = lax.broadcasted_iota(jnp.int32, (BLOCK, PROJ), 1) // HEAD_DIM
    masks = [(head_of == h) for h in range(HEADS)]

    @pl.loop(0, COL_WIDTH)
    def _(w):
        proj = mm(act_ref[w], w_ref[...])
        q_s[w] = (proj[:, :PROJ] * SCALE).astype(BF)
        k_s[w] = proj[:, PROJ : 2 * PROJ].astype(BF)
        v_s[w] = proj[:, 2 * PROJ : 3 * PROJ].astype(BF)
        g_s[w] = jax.nn.sigmoid(proj[:, 3 * PROJ :])
        dg_s[w] = mm(grad_ref[w], wo_ref[...], NT)
        dkt_s[w] = jnp.zeros((PROJ, TOKENS), F32)
        dvt_s[w] = jnp.zeros((PROJ, TOKENS), F32)

    dw_s[...] = jnp.zeros_like(dw_s)
    dwo_s[...] = jnp.zeros_like(dwo_s)

    @pl.loop(0, QBLOCKS * COL_WIDTH)
    def _(t):
        b, w = t // COL_WIDTH, lax.rem(t, COL_WIDTH)
        rows = pl.ds(pl.multiple_of(b * BLOCK, BLOCK), BLOCK)
        kbs = [pl.multiple_of(kb_ref[b, s] * BLOCK, BLOCK) for s in range(SLOTS)]
        q = q_s[w, rows, :]
        ks = [k_s[w, pl.ds(kb, BLOCK), :] for kb in kbs]
        vs = [v_s[w, pl.ds(kb, BLOCK), :] for kb in kbs]
        zero = jnp.zeros((BLOCK, PROJ), BF)
        one = jnp.ones((BLOCK, PROJ), BF)
        k4 = jnp.concatenate([jnp.where(m, x, zero) for m in masks for x in ks], axis=0)
        v4 = jnp.concatenate([jnp.where(m, x, zero) for m in masks for x in vs], axis=0)
        m4 = jnp.concatenate([jnp.where(m, one, zero) for m in masks for _ in vs], axis=0)
        vm4 = jnp.concatenate([v4, m4], axis=1)
        scores = mm(q, k4, NT) + bias_ref[rows, :].astype(F32)
        es = []
        for h in range(HEADS):
            sh = scores[:, h * WIDE : (h + 1) * WIDE]
            es.append(jnp.exp(sh - jnp.max(sh, axis=1, keepdims=True)))
        e = jnp.concatenate(es, axis=1)
        e_low = e.astype(BF)
        both = mm(e_low, vm4)
        inv = 1.0 / both[:, PROJ:]
        att = both[:, :PROJ] * inv
        g = g_s[w, rows, :]
        dg = dg_s[w, rows, :]
        gated_s[w, rows, :] = (g * att).astype(BF)
        datt = dg * g
        dgp_s[w, rows, :] = (datt * att * (1.0 - g)).astype(BF)
        datt_n = (datt * inv).astype(BF)
        prod = datt_n.astype(F32) * att
        dp = mm(datt_n, v4, NT)
        dss = []
        for h in range(HEADS):
            delta = jnp.sum(jnp.where(masks[h], prod, 0.0), axis=1, keepdims=True)
            dss.append(es[h] * (dp[:, h * WIDE : (h + 1) * WIDE] - delta))
        ds = jnp.concatenate(dss, axis=1)
        ds_low = ds.astype(BF)

        @pl.when(w == 0)
        def _():
            dacc_s[...] = ds

        @pl.when((w > 0) & (w < COL_WIDTH - 1))
        def _():
            dacc_s[...] += ds

        @pl.when(w == COL_WIDTH - 1)
        def _():
            dbias_ref[rows, :] = (dacc_s[...] + ds).astype(BF)

        dq_s[w, rows, :] = (mm(ds_low, k4) * SCALE).astype(BF)
        qt = q.astype(F32).T.astype(BF)
        dt = datt_n.astype(F32).T.astype(BF)
        dk, dv = [], []
        for h in range(HEADS):
            hs = slice(h * HEAD_DIM, (h + 1) * HEAD_DIM)
            ws = slice(h * WIDE, (h + 1) * WIDE)
            dk.append(mm(qt[hs], ds_low[:, ws]))
            dv.append(mm(dt[hs], e_low[:, ws]))
        dk = jnp.concatenate(dk, axis=0)
        dv = jnp.concatenate(dv, axis=0)
        for s in range(SLOTS):
            lanes = pl.ds(kbs[s], BLOCK)
            dkt_s[w, :, lanes] += dk[:, s * BLOCK : (s + 1) * BLOCK]
            dvt_s[w, :, lanes] += dv[:, s * BLOCK : (s + 1) * BLOCK]

    @pl.loop(0, COL_WIDTH)
    def _(w):
        dk = dkt_s[w].T.astype(BF)
        dv = dvt_s[w].T.astype(BF)
        grads = jnp.concatenate([dq_s[w], dk, dv, dgp_s[w]], axis=1)
        dpair_ref[w] = mm(grads, w_ref[...], NT).astype(BF)
        xt = act_ref[w].astype(F32).T.astype(BF)
        dw_s[...] += mm(xt, grads)
        gt = gated_s[w].astype(F32).T.astype(BF)
        dwo_s[...] += mm(gt, grad_ref[w])

    for n in range(4):
        dw_ref[n * PROJ : (n + 1) * PROJ, :] = dw_s[:, n * PROJ : (n + 1) * PROJ].astype(BF)
    dw_ref[4 * PROJ :, :] = dwo_s[...].astype(BF)


def compute(key_blocks, acol, gcol, full, w_all, w_out):
    smem = pl.BlockSpec(memory_space=pltpu.SMEM)
    vmem = pl.BlockSpec(memory_space=pltpu.VMEM)
    cols = (COL_WIDTH, TOKENS, PROJ)
    return pl.pallas_call(
        main_kernel,
        out_shape=(
            jax.ShapeDtypeStruct(cols, BF),
            jax.ShapeDtypeStruct((TOKENS, ALL), BF),
            jax.ShapeDtypeStruct((WROWS, PROJ), BF),
        ),
        in_specs=[smem] + [vmem] * 5,
        out_specs=(vmem, vmem, vmem),
        scratch_shapes=[
            pltpu.VMEM(cols, BF), pltpu.VMEM(cols, BF), pltpu.VMEM(cols, BF),
            pltpu.VMEM(cols, F32), pltpu.VMEM(cols, F32),
            pltpu.VMEM(cols, BF), pltpu.VMEM(cols, BF), pltpu.VMEM(cols, BF),
            pltpu.VMEM((COL_WIDTH, PROJ, TOKENS), F32), pltpu.VMEM((COL_WIDTH, PROJ, TOKENS), F32),
            pltpu.VMEM((BLOCK, ALL), F32),
            pltpu.VMEM((PROJ, 4 * PROJ), F32), pltpu.VMEM((PROJ, PROJ), F32),
        ],
        name="attend_back",
    )(key_blocks, acol, gcol, full, w_all, w_out)


def out_kernel(
    kb_ref, len_ref, dpair_ref, part_ref, dw_ref, dp_ref, db_ref, wsum_ref,
    r1, s1, r2, s2, r3, dense, r4, r5, s6, w6,
    sd, rd, a1, b1, a2, b2, a3, b3, a4, b4, a5, b5, a6, b6, a7, b7, sl,
):
    r, c = lax.axis_index("row"), lax.axis_index("col")
    y, zh, core = c // 4, lax.rem(c // 2, 2), lax.rem(c, 2)
    greet(r, c, COL_OFFS)
    sib = col_peer(c, (0, 0, 1))
    c1 = []
    for n in range(8):
        yy = lax.rem(y + 1 + n // 2, 4)
        cc = yy * 4 + (n % 2) * 2
        src = part_ref.at[pl.ds((cc + 1 - core) * TILE_COLS, TILE_COLS), :]
        cp = remote(src, r1.at[n], a1.at[n], b1.at[n], r, sib)
        cp.start()
        c1.append(cp)
    c5 = []
    for n, off in enumerate(ROW_OFFS):
        p = row_peer(r, off)
        cp = remote(dw_ref.at[pl.ds(p * WPART, WPART), :], r5.at[n], a5.at[n], b5.at[n], p, c)
        cp.start()
        c5.append(cp)
    cd = []
    mycols = pl.ds(r * COL_WIDTH, COL_WIDTH)
    for n, off in enumerate(ROW_OFFS):
        p = row_peer(r, off)
        src = dpair_ref.at[:, pl.ds(p * TILE_ROWS, TILE_ROWS), :]
        cp = remote(src, dp_ref.at[mycols], sd.at[n], rd.at[n], p, c)
        cp.start()
        cd.append(cp)
    ld = pltpu.make_async_copy(
        dpair_ref.at[:, pl.ds(r * TILE_ROWS, TILE_ROWS), :], dp_ref.at[mycols], sl.at[0]
    )
    ld.start()
    c2 = []
    for n in range(8):
        c1[n].wait_recv()
        yy = lax.rem(y + 1 + n // 2, 4)
        cc = yy * 4 + (n % 2) * 2 + core
        own = part_ref[pl.ds(cc * TILE_COLS, TILE_COLS), :]
        s1[n] = (own.astype(F32) + r1[n].astype(F32)).astype(BF)
        if n < 6 and n % 2 == 1:
            m = n // 2
            cp = remote(
                s1.at[pl.ds(2 * m, 2)], r2.at[m], a2.at[m], b2.at[m], r, col_peer(c, (m + 1, 0, 0))
            )
            cp.start()
            c2.append(cp)
    for cp in c5:
        cp.wait_recv()
    tot = dw_ref[pl.ds(r * WPART, WPART), :].astype(F32)
    for n in range(7):
        tot = tot + r5[n].astype(F32)
    s6[...] = tot.astype(BF)
    w6[c] = s6[...]
    c6 = []
    for n, off in enumerate(COL_OFFS):
        cp = remote(s6, w6.at[c], a6.at[n], b6.at[n], r, col_peer(c, off))
        cp.start()
        c6.append(cp)
    for cp in c2:
        cp.wait_recv()
    other = 1 - zh
    acc = s1[6 + other].astype(F32)
    for m in range(3):
        acc = acc + r2[m, other].astype(F32)
    s2[...] = acc.astype(BF)
    c3 = remote(s2, r3, a3.at[0], b3.at[0], r, col_peer(c, (0, 1, 0)))
    c3.start()
    acc = s1[6 + zh].astype(F32)
    for m in range(3):
        acc = acc + r2[m, zh].astype(F32)
    for cp in c6:
        cp.wait_recv()
    tot = w6[0].astype(F32)
    for n in range(1, COLS):
        tot = tot + w6[n].astype(F32)
    myrows = pl.ds(r * WPART, WPART)
    wsum_ref[myrows, :] = tot
    c7 = []
    for n, off in enumerate(ROW_OFFS):
        cp = remote(
            wsum_ref.at[myrows, :], wsum_ref.at[myrows, :], a7.at[n], b7.at[n], row_peer(r, off), c
        )
        cp.start()
        c7.append(cp)
    c3.wait_recv()
    acc = acc + r3[...].astype(F32)
    turned = []
    for s in range(SLOTS):
        tile = jnp.concatenate(
            [acc[:, h * WIDE + s * BLOCK : h * WIDE + (s + 1) * BLOCK] for h in range(HEADS)], axis=0
        )
        turned.append(tile.T)
    for k in range(QBLOCKS):
        val = jnp.zeros((BLOCK, PROJ), F32)
        for s in range(SLOTS):
            hit = (kb_ref[y, s] == k) & (s < len_ref[y])
            val = val + jnp.where(hit, turned[s], 0.0)
        dense[k * BLOCK : (k + 1) * BLOCK, :] = val.astype(BF)
    c4 = []
    for n, off in enumerate(ROW_OFFS):
        p = row_peer(r, off)
        cp = remote(dense.at[pl.ds(p * TILE_ROWS, TILE_ROWS), :], r4.at[n], a4.at[n], b4.at[n], p, c)
        cp.start()
        c4.append(cp)
    val = dense[pl.ds(r * TILE_ROWS, TILE_ROWS), :].astype(F32)
    for n in range(7):
        c4[n].wait_recv()
        val = val + r4[n].astype(F32)
    db_ref[...] = val
    for cp in c7 + cd:
        cp.wait_recv()
    for cp in c1 + c2 + [c3] + c4 + c5 + c6 + c7 + cd:
        cp.wait_send()
    ld.wait()


def send_out(key_blocks, list_len, dpair, part, dw):
    any_ = pl.BlockSpec(memory_space=pl.ANY)
    smem = pl.BlockSpec(memory_space=pltpu.SMEM)
    vmem = pl.BlockSpec(memory_space=pltpu.VMEM)
    dma = pltpu.SemaphoreType.DMA
    piece = (TILE_COLS, ALL)
    return pl.pallas_call(
        out_kernel,
        out_shape=(
            jax.ShapeDtypeStruct((TILE_COLS, TILE_ROWS, PROJ), BF),
            jax.ShapeDtypeStruct((TILE_ROWS, PROJ), F32),
            jax.ShapeDtypeStruct((WROWS, PROJ), F32),
        ),
        in_specs=[smem, smem, any_, vmem, vmem],
        out_specs=(any_, vmem, vmem),
        scratch_shapes=[
            pltpu.VMEM((8, *piece), BF), pltpu.VMEM((8, *piece), BF),
            pltpu.VMEM((3, 2, *piece), BF), pltpu.VMEM(piece, BF), pltpu.VMEM(piece, BF),
            pltpu.VMEM((TOKENS, PROJ), BF), pltpu.VMEM((7, TILE_ROWS, PROJ), BF),
            pltpu.VMEM((7, WPART, PROJ), BF), pltpu.VMEM((WPART, PROJ), BF),
            pltpu.VMEM((COLS, WPART, PROJ), BF),
            dma((7,)), dma((7,)), dma((8,)), dma((8,)), dma((3,)), dma((3,)), dma((1,)), dma((1,)),
            dma((7,)), dma((7,)), dma((7,)), dma((7,)), dma((15,)), dma((15,)), dma((7,)), dma((7,)),
            dma((1,)),
        ],
        compiler_params=pltpu.CompilerParams(collective_id=1, has_side_effects=True),
        name="send_out",
    )(key_blocks, list_len, dpair, part, dw)


def on_device(
    pair_act, out_grad, tri_bias, w_query, w_key, w_value, w_gate, w_out, key_blocks, list_len
):
    act = jnp.transpose(pair_act, (1, 0, 2))
    grad = jnp.transpose(out_grad, (1, 0, 2))
    bias = jnp.transpose(tri_bias, (1, 0, 2)).reshape(TILE_ROWS, PROJ)
    w_all = jnp.concatenate([w_query, w_key, w_value, w_gate], axis=1)
    acol, gcol, full = gather_in(key_blocks, list_len, act, grad, bias)
    dpair, part, dw = compute(key_blocks, acol, gcol, full, w_all, w_out)
    dp, db, ws = send_out(key_blocks, list_len, dpair, part, dw)
    d_pair = jnp.transpose(dp, (1, 0, 2))
    d_bias = jnp.transpose(db.reshape(TILE_ROWS, HEADS, TILE_COLS), (1, 0, 2))
    return (d_pair, d_bias) + tuple(ws[n * PROJ : (n + 1) * PROJ] for n in range(5))


def solution(mesh):
    in_specs = (
        P("row", "col", None), P("row", "col", None), P(None, "row", "col"),
        P(), P(), P(), P(), P(), P(), P(),
    )
    out_specs = (P("row", "col", None), P(None, "row", "col"), P(), P(), P(), P(), P())
    return jax.shard_map(
        on_device, mesh=mesh, in_specs=in_specs, out_specs=out_specs, check_vma=False
    )
```

```python
import jax
import jax.numpy as jnp
from jax import lax
from jax.experimental import pallas as pl
from jax.experimental.pallas import tpu as pltpu
from jax.sharding import PartitionSpec as P

BF = jnp.bfloat16
F32 = jnp.float32
HEADS = 4
HEAD_DIM = 32
PROJ = HEADS * HEAD_DIM
BLOCK = 128
QBLOCKS = 4
SLOTS = 3
TOKENS = QBLOCKS * BLOCK
WIDE = SLOTS * BLOCK
ROWS = 8
COLS = 16
TILE_ROWS = TOKENS // ROWS
TILE_COLS = TOKENS // COLS
COL_WIDTH = TILE_COLS // ROWS
WROWS = 5 * PROJ
WPART = WROWS // ROWS
DEAD = -1e30
UNROLL = 1
SCALE = HEAD_DIM ** -0.5

ROW_OFFS = [(dz, dx) for dz in range(2) for dx in range(4)][1:]
COL_OFFS = [(dy, dz, dc) for dy in range(4) for dz in range(2) for dc in range(2)][1:]


def row_peer(r, off):
    z, x = r // 4, lax.rem(r, 4)
    return lax.rem(z + off[0], 2) * 4 + lax.rem(x + off[1], 4)


def col_peer(c, off):
    y, z, k = c // 4, lax.rem(c // 2, 2), lax.rem(c, 2)
    return lax.rem(y + off[0], 4) * 4 + lax.rem(z + off[1], 2) * 2 + lax.rem(k + off[2], 2)


def remote(src, dst, ssem, rsem, r, c):
    return pltpu.make_async_remote_copy(
        src_ref=src,
        dst_ref=dst,
        send_sem=ssem,
        recv_sem=rsem,
        device_id=(r, c),
        device_id_type=pl.DeviceIdType.MESH,
    )


def greet(r, c, col_offs):
    sem = pltpu.get_barrier_semaphore()
    for off in ROW_OFFS:
        pl.semaphore_signal(
            sem, inc=1, device_id=(row_peer(r, off), c), device_id_type=pl.DeviceIdType.MESH
        )
    for off in col_offs:
        pl.semaphore_signal(
            sem, inc=1, device_id=(r, col_peer(c, off)), device_id_type=pl.DeviceIdType.MESH
        )
    pl.semaphore_wait(sem, len(ROW_OFFS) + len(col_offs))


IN_COLS = [(0, 0, 1), (0, 1, 0), (1, 0, 0), (2, 0, 0), (3, 0, 0)]


def in_kernel(
    kb_ref, len_ref, act_ref, grad_ref, bias_ref, acol_ref, gcol_ref, full_ref,
    got, turned, mine, sa, ra, sg, rg, sb, rb, sz, rz, sc, rc, sy, ry, sf, rf, sl,
):
    r, c = lax.axis_index("row"), lax.axis_index("col")
    y = c // 4
    greet(r, c, IN_COLS)
    first = []
    for n, off in enumerate(ROW_OFFS):
        p = row_peer(r, off)
        cp = remote(bias_ref, got.at[r], sb.at[n], rb.at[n], p, c)
        cp.start()
        first.append(cp)
    rows = pl.ds(r * TILE_ROWS, TILE_ROWS)
    big = []
    for n, off in enumerate(ROW_OFFS):
        p = row_peer(r, off)
        part = pl.ds(p * COL_WIDTH, COL_WIDTH)
        ca = remote(act_ref.at[part], acol_ref.at[:, rows, :], sa.at[n], ra.at[n], p, c)
        cg = remote(grad_ref.at[part], gcol_ref.at[:, rows, :], sg.at[n], rg.at[n], p, c)
        ca.start()
        cg.start()
        big += [ca, cg]
    own = pl.ds(r * COL_WIDTH, COL_WIDTH)
    la = pltpu.make_async_copy(act_ref.at[own], acol_ref.at[:, rows, :], sl.at[0])
    lg = pltpu.make_async_copy(grad_ref.at[own], gcol_ref.at[:, rows, :], sl.at[1])
    la.start()
    lg.start()
    got[r] = bias_ref[...]
    for cp in first:
        cp.wait()
    for k in range(QBLOCKS):
        pair = jnp.concatenate([got[2 * k], got[2 * k + 1]], axis=0).astype(F32)
        turned[k] = pair.T.astype(BF)
    for s in range(SLOTS):
        tile = turned[kb_ref[y, s]]
        tile = jnp.where(s < len_ref[y], tile.astype(F32), DEAD).astype(BF)
        mine[:, :, s * BLOCK : (s + 1) * BLOCK] = tile.reshape(HEADS, TILE_COLS, BLOCK)

    def piece(cc):
        at = pl.multiple_of(lax.rem(cc, 4) * TILE_COLS, TILE_COLS)
        return full_ref.at[cc // 4, :, pl.ds(at, TILE_COLS), :]

    sends = []
    zc = col_peer(c, (0, 1, 0))
    sib = col_peer(c, (0, 0, 1))
    cz = remote(mine, piece(c), sz.at[0], rz.at[0], r, zc)
    cz.start()
    to_y = []
    for n in range(3):
        cp = remote(mine, piece(c), sy.at[n], ry.at[n], r, col_peer(c, (n + 1, 0, 0)))
        cp.start()
        to_y.append(cp)
    cs = remote(mine, piece(c), sc.at[0], rc.at[0], r, sib)
    cs.start()
    lm = pltpu.make_async_copy(mine, piece(c), sl.at[2])
    lm.start()

    def forward(n, cc):
        cp = remote(piece(cc), piece(cc), sf.at[n], rf.at[n], r, sib)
        cp.start()
        sends.append(cp)

    cz.wait_recv()
    for n in range(3):
        cp = remote(piece(zc), piece(zc), sy.at[3 + n], ry.at[3 + n], r, col_peer(c, (n + 1, 0, 0)))
        cp.start()
        to_y.append(cp)
    forward(0, zc)
    for n in range(3):
        to_y[n].wait_recv()
        forward(1 + n, col_peer(c, (3 - n, 0, 0)))
    for n in range(3):
        to_y[3 + n].wait_recv()
        forward(4 + n, col_peer(c, (3 - n, 1, 0)))
    cz.wait_send()
    for cp in to_y:
        cp.wait_send()
    cs.wait()
    for cp in sends:
        cp.wait()
    for cp in big:
        cp.wait()
    la.wait()
    lg.wait()
    lm.wait()


def gather_in(key_blocks, list_len, act, grad, bias):
    any_ = pl.BlockSpec(memory_space=pl.ANY)
    smem = pl.BlockSpec(memory_space=pltpu.SMEM)
    vmem = pl.BlockSpec(memory_space=pltpu.VMEM)
    dma = pltpu.SemaphoreType.DMA
    return pl.pallas_call(
        in_kernel,
        out_shape=(
            jax.ShapeDtypeStruct((COL_WIDTH, TOKENS, PROJ), BF),
            jax.ShapeDtypeStruct((COL_WIDTH, TOKENS, PROJ), BF),
            jax.ShapeDtypeStruct((QBLOCKS, HEADS, BLOCK, WIDE), BF),
        ),
        in_specs=[smem, smem, any_, any_, vmem],
        out_specs=(any_, any_, any_),
        scratch_shapes=[
            pltpu.VMEM((ROWS, TILE_ROWS, PROJ), BF),
            pltpu.VMEM((QBLOCKS, PROJ, BLOCK), BF),
            pltpu.VMEM((HEADS, TILE_COLS, WIDE), BF),
            dma((7,)), dma((7,)), dma((7,)), dma((7,)), dma((7,)), dma((7,)),
            dma((1,)), dma((1,)), dma((1,)), dma((1,)), dma((6,)), dma((6,)), dma((7,)), dma((7,)),
            dma((3,)),
        ],
        compiler_params=pltpu.CompilerParams(collective_id=0, has_side_effects=True),
        name="gather_in",
    )(key_blocks, list_len, act, grad, bias)


NT = (((1,), (1,)), ((), ()))
NN = (((1,), (0,)), ((), ()))


def mm(a, b, dims=NN):
    return lax.dot_general(a, b, dims, preferred_element_type=F32)


def main_kernel(
    kb_ref, len_ref, act_ref, grad_ref, bias_ref, wq_ref, wk_ref, wv_ref, wg_ref, wo_ref,
    dpair_ref, dbias_ref, dw_ref,
    wt_s, q4_s, qt_s, kt_s, vt_s, k_s, v_s, gt_s, dgt_s, dqt_s, dgp_s, gated_s, dk_s, dv_s,
    bias_s, dacc_s, dw_s, dwo_s,
):
    for n, ref in enumerate((wq_ref, wk_ref, wv_ref, wg_ref)):
        wt_s[n * PROJ : (n + 1) * PROJ, :] = ref[...].astype(F32).T.astype(BF)
    dw_s[...] = jnp.zeros_like(dw_s)
    dwo_s[...] = jnp.zeros_like(dwo_s)

    @pl.loop(0, QBLOCKS)
    def _(b):
        for h in range(HEADS):
            bias_s[b, :, h * BLOCK : (h + 1) * BLOCK] = bias_ref[b, h].astype(F32).T

    @pl.loop(0, COL_WIDTH)
    def _(w):
        project(act_ref, grad_ref, wk_ref, wv_ref, wo_ref, wt_s, q4_s, qt_s, kt_s, vt_s, k_s, v_s,
                gt_s, dgt_s, w)

    @pl.loop(0, QBLOCKS)
    def _(b):
        kbs = [kb_ref[b, s] for s in range(SLOTS)]
        dacc_s[...] = jnp.zeros_like(dacc_s)

        @pl.loop(0, COL_WIDTH // UNROLL)
        def _(t):
            for u in range(UNROLL):
                one_pair(kbs, bias_s, q4_s, qt_s, kt_s, vt_s, k_s, v_s, gt_s, dgt_s, dqt_s, dgp_s,
                         gated_s, dk_s, dv_s, dacc_s, t * UNROLL + u, b)

        for h in range(HEADS):
            dbias_ref[b, h] = dacc_s[:, h * BLOCK : (h + 1) * BLOCK].T.astype(BF)

    @pl.loop(0, COL_WIDTH)
    def _(w):
        finish(kb_ref, len_ref, act_ref, grad_ref, wt_s, dqt_s, dgp_s, gated_s, dk_s, dv_s, dw_s,
               dwo_s, dpair_ref, w)

    for n in range(4):
        rows = slice(n * PROJ, (n + 1) * PROJ)
        dw_ref[rows, :] = dw_s[rows, :].T.astype(BF)
    dw_ref[4 * PROJ :, :] = dwo_s[...].astype(BF)


def head_rows(x):
    head_of = lax.broadcasted_iota(jnp.int32, x.shape, 0) // HEAD_DIM
    return jnp.concatenate(
        [jnp.where(head_of == h, x, jnp.zeros_like(x)) for h in range(HEADS)], axis=1
    )


def project(act_ref, grad_ref, wk_ref, wv_ref, wo_ref, wt_s, q4_s, qt_s, kt_s, vt_s, k_s, v_s,
            gt_s, dgt_s, w):
    x = act_ref[w]
    turned = mm(wt_s[...], x, NT)
    qt = (turned[:PROJ] * SCALE).astype(BF)
    kt = turned[PROJ : 2 * PROJ].astype(BF)
    vt = turned[2 * PROJ : 3 * PROJ].astype(BF)
    for b in range(QBLOCKS):
        cols = slice(b * BLOCK, (b + 1) * BLOCK)
        qt_s[w, b] = qt[:, cols]
        q4_s[w, b] = head_rows(qt[:, cols])
        kt_s[w, b] = kt[:, cols]
        vt_s[w, b] = vt[:, cols]
        gt_s[w, b] = jax.nn.sigmoid(turned[3 * PROJ :, cols])
    dgt = mm(wo_ref[...], grad_ref[w], NT)
    k = mm(x, wk_ref[...]).astype(BF)
    v = mm(x, wv_ref[...]).astype(BF)
    for b in range(QBLOCKS):
        rows = slice(b * BLOCK, (b + 1) * BLOCK)
        dgt_s[w, b] = dgt[:, rows]
        k_s[w, b] = k[rows]
        v_s[w, b] = v[rows]


def one_pair(kbs, bias_s, q4_s, qt_s, kt_s, vt_s, k_s, v_s, gt_s, dgt_s, dqt_s, dgp_s, gated_s,
             dk_s, dv_s, dacc_s, w, b):
    def chosen(ref, axis):
        return jnp.concatenate([ref[w, kb] for kb in kbs], axis=axis)

    heads = [slice(h * BLOCK, (h + 1) * BLOCK) for h in range(HEADS)]
    scores = mm(chosen(k_s, 0), q4_s[w, b]) + bias_s[b]
    e = jnp.exp(scores - jnp.max(scores, axis=0, keepdims=True))
    e_low = e.astype(BF)
    vt = chosen(vt_s, 1)
    ones = jnp.ones((16, WIDE), BF)
    atts, invs = [], []
    for h in range(0, HEADS, 2):
        lhs = jnp.concatenate([vt[h * HEAD_DIM : (h + 2) * HEAD_DIM], ones], axis=0)
        both = mm(lhs, e_low[:, h * BLOCK : (h + 2) * BLOCK])
        inv = 1.0 / both[2 * HEAD_DIM : 2 * HEAD_DIM + 1]
        for n in range(2):
            part = inv[:, n * BLOCK : (n + 1) * BLOCK]
            raw = both[n * HEAD_DIM : (n + 1) * HEAD_DIM, n * BLOCK : (n + 1) * BLOCK]
            atts.append(raw * part)
            invs.append(jnp.broadcast_to(part, (HEAD_DIM, BLOCK)))
    att = jnp.concatenate(atts, axis=0)
    inv = jnp.concatenate(invs, axis=0)
    g = gt_s[w, b]
    datt = dgt_s[w, b] * g
    gated_s[w, b] = (g * att).astype(BF)
    dgp_s[w, b] = (datt * att * (1.0 - g)).astype(BF)
    dn = (datt * inv).astype(BF)
    prod = dn.astype(F32) * att
    delta = jnp.concatenate(
        [
            jnp.sum(prod[h * HEAD_DIM : (h + 1) * HEAD_DIM], axis=0, keepdims=True)
            for h in range(HEADS)
        ],
        axis=1,
    )
    ds = e * (mm(chosen(v_s, 0), head_rows(dn)) - delta)
    dacc_s[...] += ds
    ds_low = ds.astype(BF)
    kt = chosen(kt_s, 1)
    qt = qt_s[w, b]
    for h in range(HEADS):
        hs = slice(h * HEAD_DIM, (h + 1) * HEAD_DIM)
        dqt_s[w, b, hs, :] = (mm(kt[hs], ds_low[:, heads[h]]) * SCALE).astype(BF)
        dk = mm(qt[hs], ds_low[:, heads[h]], NT)
        dv = mm(dn[hs], e_low[:, heads[h]], NT)
        for s in range(SLOTS):
            dk_s[w, b, s, hs, :] = dk[:, s * BLOCK : (s + 1) * BLOCK]
            dv_s[w, b, s, hs, :] = dv[:, s * BLOCK : (s + 1) * BLOCK]


def finish(kb_ref, len_ref, act_ref, grad_ref, wt_s, dqt_s, dgp_s, gated_s, dk_s, dv_s, dw_s, dwo_s,
           dpair_ref, w):
    dks, dvs = [], []
    for k in range(QBLOCKS):
        dk = jnp.zeros((PROJ, BLOCK), F32)
        dv = jnp.zeros((PROJ, BLOCK), F32)
        for b in range(QBLOCKS):
            slot = jnp.int32(SLOTS)
            for s in range(SLOTS):
                slot = jnp.where((kb_ref[b, s] == k) & (s < len_ref[b]), s, slot)
            listed = slot < SLOTS
            at = jnp.minimum(slot, SLOTS - 1)
            dk = dk + jnp.where(listed, dk_s[w, b, at], 0.0)
            dv = dv + jnp.where(listed, dv_s[w, b, at], 0.0)
        dks.append(dk.astype(BF))
        dvs.append(dv.astype(BF))
    parts = [
        jnp.concatenate([dqt_s[w, b] for b in range(QBLOCKS)], axis=1),
        jnp.concatenate(dks, axis=1),
        jnp.concatenate(dvs, axis=1),
        jnp.concatenate([dgp_s[w, b] for b in range(QBLOCKS)], axis=1),
    ]
    grads = jnp.concatenate(parts, axis=0)
    dw_s[...] += mm(grads, act_ref[w])
    gated = jnp.concatenate([gated_s[w, b] for b in range(QBLOCKS)], axis=1)
    dwo_s[...] += mm(gated, grad_ref[w])
    dpair_ref[w] = lax.dot_general(
        grads, wt_s[...], (((0,), (0,)), ((), ())), preferred_element_type=F32
    ).astype(BF)


def compute(key_blocks, list_len, acol, gcol, full, *weights):
    smem = pl.BlockSpec(memory_space=pltpu.SMEM)
    vmem = pl.BlockSpec(memory_space=pltpu.VMEM)
    cols = (COL_WIDTH, TOKENS, PROJ)
    tiles = (COL_WIDTH, QBLOCKS, PROJ, BLOCK)
    slots = (COL_WIDTH, QBLOCKS, SLOTS, PROJ, BLOCK)
    return pl.pallas_call(
        main_kernel,
        out_shape=(
            jax.ShapeDtypeStruct(cols, BF),
            jax.ShapeDtypeStruct((QBLOCKS, HEADS, BLOCK, WIDE), BF),
            jax.ShapeDtypeStruct((WROWS, PROJ), BF),
        ),
        in_specs=[smem] * 2 + [vmem] * 8,
        out_specs=(vmem, vmem, vmem),
        scratch_shapes=[
            pltpu.VMEM((4 * PROJ, PROJ), BF),
            pltpu.VMEM((COL_WIDTH, QBLOCKS, PROJ, HEADS * BLOCK), BF),
            pltpu.VMEM(tiles, BF), pltpu.VMEM(tiles, BF), pltpu.VMEM(tiles, BF),
            pltpu.VMEM(tiles, BF), pltpu.VMEM(tiles, BF),
            pltpu.VMEM(tiles, F32), pltpu.VMEM(tiles, F32),
            pltpu.VMEM(tiles, BF), pltpu.VMEM(tiles, BF), pltpu.VMEM(tiles, BF),
            pltpu.VMEM(slots, F32), pltpu.VMEM(slots, F32),
            pltpu.VMEM((QBLOCKS, WIDE, HEADS * BLOCK), F32),
            pltpu.VMEM((WIDE, HEADS * BLOCK), F32),
            pltpu.VMEM((4 * PROJ, PROJ), F32), pltpu.VMEM((PROJ, PROJ), F32),
        ],
        name="attend_back",
    )(key_blocks, list_len, acol, gcol, full, *weights)


def out_kernel(
    kb_ref, len_ref, dpair_ref, part_ref, dw_ref, dp_ref, db_ref, wsum_ref,
    r1, s1, r2, s2, r3, dense, r4, r5, s6, w6,
    sd, rd, a1, b1, a2, b2, a3, b3, a4, b4, a5, b5, a6, b6, a7, b7, sl,
):
    r, c = lax.axis_index("row"), lax.axis_index("col")
    y, zh, core = c // 4, lax.rem(c // 2, 2), lax.rem(c, 2)
    greet(r, c, COL_OFFS)
    sib = col_peer(c, (0, 0, 1))

    def piece(cc):
        at = pl.multiple_of(lax.rem(cc, 4) * TILE_COLS, TILE_COLS)
        return part_ref.at[cc // 4, :, pl.ds(at, TILE_COLS), :]

    c1 = []
    for n in range(8):
        yy = lax.rem(y + 1 + n // 2, 4)
        cc = yy * 4 + (n % 2) * 2
        src = piece(cc + 1 - core)
        cp = remote(src, r1.at[n], a1.at[n], b1.at[n], r, sib)
        cp.start()
        c1.append(cp)
    c5 = []
    for n, off in enumerate(ROW_OFFS):
        p = row_peer(r, off)
        cp = remote(dw_ref.at[pl.ds(p * WPART, WPART), :], r5.at[n], a5.at[n], b5.at[n], p, c)
        cp.start()
        c5.append(cp)
    cd = []
    mycols = pl.ds(r * COL_WIDTH, COL_WIDTH)
    for n, off in enumerate(ROW_OFFS):
        p = row_peer(r, off)
        src = dpair_ref.at[:, pl.ds(p * TILE_ROWS, TILE_ROWS), :]
        cp = remote(src, dp_ref.at[mycols], sd.at[n], rd.at[n], p, c)
        cp.start()
        cd.append(cp)
    ld = pltpu.make_async_copy(
        dpair_ref.at[:, pl.ds(r * TILE_ROWS, TILE_ROWS), :], dp_ref.at[mycols], sl.at[0]
    )
    ld.start()
    c2 = []
    for n in range(8):
        c1[n].wait_recv()
        yy = lax.rem(y + 1 + n // 2, 4)
        cc = yy * 4 + (n % 2) * 2 + core
        own = piece(cc)[...]
        s1[n] = (own.astype(F32) + r1[n].astype(F32)).astype(BF)
        if n < 6 and n % 2 == 1:
            m = n // 2
            cp = remote(
                s1.at[pl.ds(2 * m, 2)], r2.at[m], a2.at[m], b2.at[m], r, col_peer(c, (m + 1, 0, 0))
            )
            cp.start()
            c2.append(cp)
    for cp in c5:
        cp.wait_recv()
    tot = dw_ref[pl.ds(r * WPART, WPART), :].astype(F32)
    for n in range(7):
        tot = tot + r5[n].astype(F32)
    s6[...] = tot.astype(BF)
    w6[c] = s6[...]
    c6 = []
    for n, off in enumerate(COL_OFFS):
        cp = remote(s6, w6.at[c], a6.at[n], b6.at[n], r, col_peer(c, off))
        cp.start()
        c6.append(cp)
    for cp in c2:
        cp.wait_recv()
    other = 1 - zh
    acc = s1[6 + other].astype(F32)
    for m in range(3):
        acc = acc + r2[m, other].astype(F32)
    s2[...] = acc.astype(BF)
    c3 = remote(s2, r3, a3.at[0], b3.at[0], r, col_peer(c, (0, 1, 0)))
    c3.start()
    acc = s1[6 + zh].astype(F32)
    for m in range(3):
        acc = acc + r2[m, zh].astype(F32)
    for cp in c6:
        cp.wait_recv()
    tot = w6[0].astype(F32)
    for n in range(1, COLS):
        tot = tot + w6[n].astype(F32)
    myrows = pl.ds(r * WPART, WPART)
    wsum_ref[myrows, :] = tot
    c7 = []
    for n, off in enumerate(ROW_OFFS):
        cp = remote(
            wsum_ref.at[myrows, :], wsum_ref.at[myrows, :], a7.at[n], b7.at[n], row_peer(r, off), c
        )
        cp.start()
        c7.append(cp)
    c3.wait_recv()
    acc = acc + r3[...].astype(F32)
    turned = []
    for s in range(SLOTS):
        tile = acc[:, :, s * BLOCK : (s + 1) * BLOCK].reshape(PROJ, BLOCK)
        turned.append(tile.T)
    for k in range(QBLOCKS):
        val = jnp.zeros((BLOCK, PROJ), F32)
        for s in range(SLOTS):
            hit = (kb_ref[y, s] == k) & (s < len_ref[y])
            val = val + jnp.where(hit, turned[s], 0.0)
        dense[k * BLOCK : (k + 1) * BLOCK, :] = val.astype(BF)
    c4 = []
    for n, off in enumerate(ROW_OFFS):
        p = row_peer(r, off)
        cp = remote(dense.at[pl.ds(p * TILE_ROWS, TILE_ROWS), :], r4.at[n], a4.at[n], b4.at[n], p, c)
        cp.start()
        c4.append(cp)
    val = dense[pl.ds(r * TILE_ROWS, TILE_ROWS), :].astype(F32)
    for n in range(7):
        c4[n].wait_recv()
        val = val + r4[n].astype(F32)
    db_ref[...] = val
    for cp in c7 + cd:
        cp.wait_recv()
    for cp in c1 + c2 + [c3] + c4 + c5 + c6 + c7 + cd:
        cp.wait_send()
    ld.wait()


def send_out(key_blocks, list_len, dpair, part, dw):
    any_ = pl.BlockSpec(memory_space=pl.ANY)
    smem = pl.BlockSpec(memory_space=pltpu.SMEM)
    vmem = pl.BlockSpec(memory_space=pltpu.VMEM)
    dma = pltpu.SemaphoreType.DMA
    piece = (HEADS, TILE_COLS, WIDE)
    return pl.pallas_call(
        out_kernel,
        out_shape=(
            jax.ShapeDtypeStruct((TILE_COLS, TILE_ROWS, PROJ), BF),
            jax.ShapeDtypeStruct((TILE_ROWS, PROJ), F32),
            jax.ShapeDtypeStruct((WROWS, PROJ), F32),
        ),
        in_specs=[smem, smem, any_, vmem, vmem],
        out_specs=(any_, vmem, vmem),
        scratch_shapes=[
            pltpu.VMEM((8, *piece), BF), pltpu.VMEM((8, *piece), BF),
            pltpu.VMEM((3, 2, *piece), BF), pltpu.VMEM(piece, BF), pltpu.VMEM(piece, BF),
            pltpu.VMEM((TOKENS, PROJ), BF), pltpu.VMEM((7, TILE_ROWS, PROJ), BF),
            pltpu.VMEM((7, WPART, PROJ), BF), pltpu.VMEM((WPART, PROJ), BF),
            pltpu.VMEM((COLS, WPART, PROJ), BF),
            dma((7,)), dma((7,)), dma((8,)), dma((8,)), dma((3,)), dma((3,)), dma((1,)), dma((1,)),
            dma((7,)), dma((7,)), dma((7,)), dma((7,)), dma((15,)), dma((15,)), dma((7,)), dma((7,)),
            dma((1,)),
        ],
        compiler_params=pltpu.CompilerParams(collective_id=1, has_side_effects=True),
        name="send_out",
    )(key_blocks, list_len, dpair, part, dw)


def on_device(
    pair_act, out_grad, tri_bias, w_query, w_key, w_value, w_gate, w_out, key_blocks, list_len
):
    act = jnp.transpose(pair_act, (1, 0, 2))
    grad = jnp.transpose(out_grad, (1, 0, 2))
    bias = jnp.transpose(tri_bias, (1, 0, 2)).reshape(TILE_ROWS, PROJ)
    acol, gcol, full = gather_in(key_blocks, list_len, act, grad, bias)
    dpair, part, dw = compute(
        key_blocks, list_len, acol, gcol, full, w_query, w_key, w_value, w_gate, w_out
    )
    dp, db, ws = send_out(key_blocks, list_len, dpair, part, dw)
    d_pair = jnp.transpose(dp, (1, 0, 2))
    d_bias = jnp.transpose(db.reshape(TILE_ROWS, HEADS, TILE_COLS), (1, 0, 2))
    return (d_pair, d_bias) + tuple(ws[n * PROJ : (n + 1) * PROJ] for n in range(5))


def solution(mesh):
    in_specs = (
        P("row", "col", None), P("row", "col", None), P(None, "row", "col"),
        P(), P(), P(), P(), P(), P(), P(),
    )
    out_specs = (P("row", "col", None), P(None, "row", "col"), P(), P(), P(), P(), P())
    return jax.shard_map(
        on_device, mesh=mesh, in_specs=in_specs, out_specs=out_specs, check_vma=False
    )
```

```python
import jax
import jax.numpy as jnp
from jax import lax
from jax.experimental import pallas as pl
from jax.experimental.pallas import tpu as pltpu
from jax.sharding import PartitionSpec as P

BF = jnp.bfloat16
F32 = jnp.float32
HEADS = 4
HEAD_DIM = 32
PROJ = HEADS * HEAD_DIM
BLOCK = 128
QBLOCKS = 4
SLOTS = 3
TOKENS = QBLOCKS * BLOCK
WIDE = SLOTS * BLOCK
ROWS = 8
COLS = 16
TILE_ROWS = TOKENS // ROWS
TILE_COLS = TOKENS // COLS
COL_WIDTH = TILE_COLS // ROWS
WROWS = 5 * PROJ
WPART = WROWS // ROWS
DEAD = -1e30
SCALE = HEAD_DIM ** -0.5

ROW_OFFS = [(dz, dx) for dz in range(2) for dx in range(4)][1:]
COL_OFFS = [(dy, dz, dc) for dy in range(4) for dz in range(2) for dc in range(2)][1:]


def row_peer(r, off):
    z, x = r // 4, lax.rem(r, 4)
    return lax.rem(z + off[0], 2) * 4 + lax.rem(x + off[1], 4)


def col_peer(c, off):
    y, z, k = c // 4, lax.rem(c // 2, 2), lax.rem(c, 2)
    return lax.rem(y + off[0], 4) * 4 + lax.rem(z + off[1], 2) * 2 + lax.rem(k + off[2], 2)


def remote(src, dst, ssem, rsem, r, c):
    return pltpu.make_async_remote_copy(
        src_ref=src,
        dst_ref=dst,
        send_sem=ssem,
        recv_sem=rsem,
        device_id=(r, c),
        device_id_type=pl.DeviceIdType.MESH,
    )


NT = (((1,), (1,)), ((), ()))
NN = (((1,), (0,)), ((), ()))


def mm(a, b, dims=NN):
    return lax.dot_general(a, b, dims, preferred_element_type=F32)


def head_rows(x):
    head_of = lax.broadcasted_iota(jnp.int32, x.shape, 0) // HEAD_DIM
    return jnp.concatenate(
        [jnp.where(head_of == h, x, jnp.zeros_like(x)) for h in range(HEADS)], axis=1
    )


def project(act_ref, grad_ref, wk_ref, wv_ref, wo_ref, wt_s, q4_s, qt_s, kt_s, vt_s, k_s, v_s,
            gt_s, dgt_s, w):
    x = act_ref[w]
    turned = mm(wt_s[...], x, NT)
    qt = (turned[:PROJ] * SCALE).astype(BF)
    kt = turned[PROJ : 2 * PROJ].astype(BF)
    vt = turned[2 * PROJ : 3 * PROJ].astype(BF)
    for b in range(QBLOCKS):
        cols = slice(b * BLOCK, (b + 1) * BLOCK)
        qt_s[w, b] = qt[:, cols]
        q4_s[w, b] = head_rows(qt[:, cols])
        kt_s[w, b] = kt[:, cols]
        vt_s[w, b] = vt[:, cols]
        gt_s[w, b] = jax.nn.sigmoid(turned[3 * PROJ :, cols])
    dgt = mm(wo_ref[...], grad_ref[w], NT)
    k = mm(x, wk_ref[...]).astype(BF)
    v = mm(x, wv_ref[...]).astype(BF)
    for b in range(QBLOCKS):
        rows = slice(b * BLOCK, (b + 1) * BLOCK)
        dgt_s[w, b] = dgt[:, rows]
        k_s[w, b] = k[rows]
        v_s[w, b] = v[rows]


def one_pair(kbs, bias_s, q4_s, qt_s, kt_s, vt_s, k_s, v_s, gt_s, dgt_s, dqt_s, dgp_s, gated_s,
             dk_s, dv_s, dacc_s, w, b):
    def chosen(ref, axis):
        return jnp.concatenate([ref[w, kb] for kb in kbs], axis=axis)

    heads = [slice(h * BLOCK, (h + 1) * BLOCK) for h in range(HEADS)]
    scores = mm(chosen(k_s, 0), q4_s[w, b]) + bias_s[0]
    e = jnp.exp(scores - jnp.max(scores, axis=0, keepdims=True))
    e_low = e.astype(BF)
    vt = chosen(vt_s, 1)
    ones = jnp.ones((16, WIDE), BF)
    atts, invs = [], []
    for h in range(0, HEADS, 2):
        lhs = jnp.concatenate([vt[h * HEAD_DIM : (h + 2) * HEAD_DIM], ones], axis=0)
        both = mm(lhs, e_low[:, h * BLOCK : (h + 2) * BLOCK])
        inv = 1.0 / both[2 * HEAD_DIM : 2 * HEAD_DIM + 1]
        for n in range(2):
            part = inv[:, n * BLOCK : (n + 1) * BLOCK]
            raw = both[n * HEAD_DIM : (n + 1) * HEAD_DIM, n * BLOCK : (n + 1) * BLOCK]
            atts.append(raw * part)
            invs.append(jnp.broadcast_to(part, (HEAD_DIM, BLOCK)))
    att = jnp.concatenate(atts, axis=0)
    inv = jnp.concatenate(invs, axis=0)
    g = gt_s[w, b]
    datt = dgt_s[w, b] * g
    gated_s[w, b] = (g * att).astype(BF)
    dgp_s[w, b] = (datt * att * (1.0 - g)).astype(BF)
    dn = (datt * inv).astype(BF)
    prod = dn.astype(F32) * att
    delta = jnp.concatenate(
        [
            jnp.sum(prod[h * HEAD_DIM : (h + 1) * HEAD_DIM], axis=0, keepdims=True)
            for h in range(HEADS)
        ],
        axis=1,
    )
    ds = e * (mm(chosen(v_s, 0), head_rows(dn)) - delta)
    dacc_s[...] += ds
    ds_low = ds.astype(BF)
    kt = chosen(kt_s, 1)
    qt = qt_s[w, b]
    for h in range(HEADS):
        hs = slice(h * HEAD_DIM, (h + 1) * HEAD_DIM)
        dqt_s[w, b, hs, :] = (mm(kt[hs], ds_low[:, heads[h]]) * SCALE).astype(BF)
        dk = mm(qt[hs], ds_low[:, heads[h]], NT)
        dv = mm(dn[hs], e_low[:, heads[h]], NT)
        for s in range(SLOTS):
            dk_s[w, b, s, hs, :] = dk[:, s * BLOCK : (s + 1) * BLOCK]
            dv_s[w, b, s, hs, :] = dv[:, s * BLOCK : (s + 1) * BLOCK]


def collect(kb_ref, len_ref, act_ref, grad_ref, dqt_s, dgp_s, gated_s, dk_s, dv_s, dw_s, dwo_s,
            grads_s, w):
    dks, dvs = [], []
    for k in range(QBLOCKS):
        dk = jnp.zeros((PROJ, BLOCK), F32)
        dv = jnp.zeros((PROJ, BLOCK), F32)
        for b in range(QBLOCKS):
            slot = jnp.int32(SLOTS)
            for s in range(SLOTS):
                slot = jnp.where((kb_ref[b, s] == k) & (s < len_ref[b]), s, slot)
            listed = slot < SLOTS
            at = jnp.minimum(slot, SLOTS - 1)
            dk = dk + jnp.where(listed, dk_s[w, b, at], 0.0)
            dv = dv + jnp.where(listed, dv_s[w, b, at], 0.0)
        dks.append(dk.astype(BF))
        dvs.append(dv.astype(BF))
    parts = [
        jnp.concatenate([dqt_s[w, b] for b in range(QBLOCKS)], axis=1),
        jnp.concatenate(dks, axis=1),
        jnp.concatenate(dvs, axis=1),
        jnp.concatenate([dgp_s[w, b] for b in range(QBLOCKS)], axis=1),
    ]
    grads = jnp.concatenate(parts, axis=0)
    grads_s[w] = grads
    dw_s[...] += mm(grads, act_ref[w])
    gated = jnp.concatenate([gated_s[w, b] for b in range(QBLOCKS)], axis=1)
    dwo_s[...] += mm(gated, grad_ref[w])


class Sems:
    def __init__(self, send, recv):
        self.send, self.recv, self.used = send, recv, 0

    def remote(self, src, dst, r, c):
        n = self.used
        self.used += 1
        cp = remote(src, dst, self.send.at[n], self.recv.at[n], r, c)
        cp.start()
        return cp


N_SEMS = 56 + 28 + 24 + 29 + 24


def fused_kernel(
    kb_ref, len_ref, pair_ref, cot_ref, bias_ref, wq_ref, wk_ref, wv_ref, wg_ref, wo_ref,
    dp_ref, db_ref, wsum_ref,
    flat_s, actt, gradt, act_s, grad_s, turned, got, mine, full,
    wt_s, q4_s, qt_s, kt_s, vt_s, k_s, v_s, gt_s, dgt_s, dqt_s, dgp_s, gated_s, dk_s, dv_s,
    bias_s, dacc_s, dw_s, dwo_s, grads_s, dpair_s,
    part, r1, s1, r2, s2, r3, dense, r4, dwb, r5, s6, w6,
    send_sem, recv_sem,
):
    r, c = lax.axis_index("row"), lax.axis_index("col")
    y, zh, core = c // 4, lax.rem(c // 2, 2), lax.rem(c, 2)
    sems = Sems(send_sem, recv_sem)
    barrier = pltpu.get_barrier_semaphore()
    peers = [(row_peer(r, off), c) for off in ROW_OFFS] + [(r, col_peer(c, o)) for o in COL_OFFS]
    for peer in peers:
        pl.semaphore_signal(barrier, inc=1, device_id=peer, device_id_type=pl.DeviceIdType.MESH)

    turned[...] = bias_ref[...].astype(F32).T.astype(BF)
    for src, dst in ((pair_ref, actt), (cot_ref, gradt)):
        flat_s[...] = src[...].astype(F32).reshape(TILE_ROWS * TILE_COLS, PROJ)

        @pl.loop(0, TILE_COLS // 4)
        def _(n):
            for u in range(4):
                j = n * 4 + u
                dst[j] = flat_s[pl.ds(j, TILE_ROWS, stride=TILE_COLS), :].astype(BF)

    got[r] = turned[...]
    pl.semaphore_wait(barrier, len(peers))

    first = [sems.remote(turned, got.at[r], row_peer(r, off), c) for off in ROW_OFFS]
    rows = pl.ds(pl.multiple_of(r * TILE_ROWS, TILE_ROWS), TILE_ROWS)
    big = []
    for w in range(COL_WIDTH):
        now = []
        for off in ROW_OFFS:
            p = row_peer(r, off)
            now.append(sems.remote(actt.at[p * COL_WIDTH + w], act_s.at[w, rows, :], p, c))
            now.append(sems.remote(gradt.at[p * COL_WIDTH + w], grad_s.at[w, rows, :], p, c))
        big.append(now)
    for w in range(COL_WIDTH):
        act_s[w, rows, :] = actt[r * COL_WIDTH + w]
        grad_s[w, rows, :] = gradt[r * COL_WIDTH + w]
    for n, ref in enumerate((wq_ref, wk_ref, wv_ref, wg_ref)):
        wt_s[n * PROJ : (n + 1) * PROJ, :] = ref[...].astype(F32).T.astype(BF)
    dw_s[...] = jnp.zeros_like(dw_s)
    dwo_s[...] = jnp.zeros_like(dwo_s)

    for cp in first:
        cp.wait_recv()
    for s in range(SLOTS):
        k = kb_ref[y, s]
        tile = jnp.concatenate([got[2 * k], got[2 * k + 1]], axis=0).astype(F32)
        tile = jnp.where(s < len_ref[y], tile, DEAD).T.astype(BF)
        mine[:, :, s * BLOCK : (s + 1) * BLOCK] = tile.reshape(HEADS, TILE_COLS, BLOCK)

    def piece(ref, cc):
        at = pl.multiple_of(lax.rem(cc, 4) * TILE_COLS, TILE_COLS)
        return ref.at[cc // 4, :, pl.ds(at, TILE_COLS), :]

    zc, sib = col_peer(c, (0, 1, 0)), col_peer(c, (0, 0, 1))
    ys = [col_peer(c, (n + 1, 0, 0)) for n in range(3)]
    cz = sems.remote(mine, piece(full, c), r, zc)
    to_y = [sems.remote(mine, piece(full, c), r, ys[n]) for n in range(3)]
    cs = sems.remote(mine, piece(full, c), r, sib)
    piece(full, c)[...] = mine[...]
    cz.wait_recv()
    to_y += [sems.remote(piece(full, zc), piece(full, zc), r, ys[n]) for n in range(3)]
    fwd = [sems.remote(piece(full, zc), piece(full, zc), r, sib)]

    def column(w):
        for cp in big[w]:
            cp.wait_recv()
        project(act_s, grad_s, wk_ref, wv_ref, wo_ref, wt_s, q4_s, qt_s, kt_s, vt_s, k_s, v_s,
                gt_s, dgt_s, w)

    def pass_on(z):
        for n in range(3):
            to_y[3 * z + n].wait_recv()
            cc = col_peer(c, (3 - n, z, 0))
            fwd.append(sems.remote(piece(full, cc), piece(full, cc), r, sib))

    column(0)
    pass_on(0)
    column(1)
    pass_on(1)
    column(2)
    column(3)
    cs.wait_recv()
    for cp in fwd:
        cp.wait_recv()

    c1, c2 = [], []
    total = None

    def merge(t):
        for n in range(2):
            c1[t][n].wait_recv()
            at = pl.multiple_of((2 * n + core) * TILE_COLS, TILE_COLS)
            own = part[t, :, pl.ds(at, TILE_COLS), :]
            s1[t, n] = (own.astype(F32) + r1[t, n].astype(F32)).astype(BF)

    for t in range(QBLOCKS):
        b = lax.rem(y + 1 + t, QBLOCKS)
        kbs = [kb_ref[b, s] for s in range(SLOTS)]
        for h in range(HEADS):
            bias_s[0, :, h * BLOCK : (h + 1) * BLOCK] = full[b, h].astype(F32).T
        dacc_s[...] = jnp.zeros_like(dacc_s)

        @pl.loop(0, COL_WIDTH)
        def _(w):
            one_pair(kbs, bias_s, q4_s, qt_s, kt_s, vt_s, k_s, v_s, gt_s, dgt_s, dqt_s, dgp_s,
                     gated_s, dk_s, dv_s, dacc_s, w, b)

        for h in range(HEADS):
            part[t, h] = dacc_s[:, h * BLOCK : (h + 1) * BLOCK].T.astype(BF)
        now = []
        for n in range(2):
            at = pl.multiple_of((2 * n + 1 - core) * TILE_COLS, TILE_COLS)
            now.append(sems.remote(part.at[t, :, pl.ds(at, TILE_COLS), :], r1.at[t, n], r, sib))
        c1.append(now)
        if t > 0:
            merge(t - 1)
            c2.append(sems.remote(s1.at[t - 1], r2.at[t - 1], r, ys[t - 1]))

    @pl.loop(0, COL_WIDTH)
    def _(w):
        collect(kb_ref, len_ref, act_s, grad_s, dqt_s, dgp_s, gated_s, dk_s, dv_s, dw_s, dwo_s,
                grads_s, w)

    for n in range(4):
        at = slice(n * PROJ, (n + 1) * PROJ)
        dwb[at, :] = dw_s[at, :].T.astype(BF)
    dwb[4 * PROJ :, :] = dwo_s[...].astype(BF)
    c5 = []
    for n, off in enumerate(ROW_OFFS):
        p = row_peer(r, off)
        src = dwb.at[pl.ds(pl.multiple_of(p * WPART, 16), WPART), :]
        c5.append(sems.remote(src, r5.at[n], p, c))
    merge(3)
    for cp in c2:
        cp.wait_recv()

    def share(z):
        acc = s1[3, z].astype(F32)
        for m in range(3):
            acc = acc + r2[m, z].astype(F32)
        return acc

    s2[...] = share(1 - zh).astype(BF)
    c3 = sems.remote(s2, r3, r, zc)
    cd = []
    w_all = jnp.concatenate([ref[...] for ref in (wq_ref, wk_ref, wv_ref, wg_ref)], axis=1)
    for w in range(COL_WIDTH):
        back = mm(w_all, grads_s[w])
        for b in range(QBLOCKS):
            at = slice(b * BLOCK, (b + 1) * BLOCK)
            dpair_s[w, at, :] = back[:, at].T.astype(BF)
        for off in ROW_OFFS:
            p = row_peer(r, off)
            src = dpair_s.at[w, pl.ds(pl.multiple_of(p * TILE_ROWS, TILE_ROWS), TILE_ROWS), :]
            cd.append(sems.remote(src, dp_ref.at[r * COL_WIDTH + w], p, c))
        if w == 1:
            for cp in c5:
                cp.wait_recv()
            tot = dwb[pl.ds(pl.multiple_of(r * WPART, 16), WPART), :].astype(F32)
            for n in range(7):
                tot = tot + r5[n].astype(F32)
            s6[...] = tot.astype(BF)
            w6[c] = s6[...]
            c6 = [sems.remote(s6, w6.at[c], r, col_peer(c, off)) for off in COL_OFFS]
    for w in range(COL_WIDTH):
        dp_ref[r * COL_WIDTH + w] = dpair_s[w, rows, :]
    acc = share(zh)
    c3.wait_recv()
    acc = acc + r3[...].astype(F32)
    tiles = [
        acc[:, :, s * BLOCK : (s + 1) * BLOCK].reshape(PROJ, BLOCK).T for s in range(SLOTS)
    ]
    for k in range(QBLOCKS):
        val = jnp.zeros((BLOCK, PROJ), F32)
        for s in range(SLOTS):
            hit = (kb_ref[y, s] == k) & (s < len_ref[y])
            val = val + jnp.where(hit, tiles[s], 0.0)
        dense[k * BLOCK : (k + 1) * BLOCK, :] = val.astype(BF)
    c4 = []
    for n, off in enumerate(ROW_OFFS):
        p = row_peer(r, off)
        src = dense.at[pl.ds(pl.multiple_of(p * TILE_ROWS, TILE_ROWS), TILE_ROWS), :]
        c4.append(sems.remote(src, r4.at[n], p, c))
    for cp in c6:
        cp.wait_recv()
    tot = w6[0].astype(F32)
    for n in range(1, COLS):
        tot = tot + w6[n].astype(F32)
    myrows = pl.ds(pl.multiple_of(r * WPART, 16), WPART)
    wsum_ref[myrows, :] = tot
    c7 = [
        sems.remote(wsum_ref.at[myrows, :], wsum_ref.at[myrows, :], row_peer(r, off), c)
        for off in ROW_OFFS
    ]
    val = dense[rows, :].astype(F32)
    for n in range(7):
        c4[n].wait_recv()
        val = val + r4[n].astype(F32)
    db_ref[...] = val.T
    for cp in cd + c7:
        cp.wait_recv()
    for cp in sum(big, []) + first + [cz, cs, c3] + to_y + fwd + sum(c1, []) + c2 + c4 + c5 + c6 + c7 + cd:
        cp.wait_send()


def fused(key_blocks, list_len, act, grad, bias, *weights):
    any_ = pl.BlockSpec(memory_space=pl.ANY)
    smem = pl.BlockSpec(memory_space=pltpu.SMEM)
    vmem = pl.BlockSpec(memory_space=pltpu.VMEM)
    dma = pltpu.SemaphoreType.DMA
    flip = (TILE_COLS, TILE_ROWS, PROJ)
    cols = (COL_WIDTH, TOKENS, PROJ)
    tiles = (COL_WIDTH, QBLOCKS, PROJ, BLOCK)
    slots = (COL_WIDTH, QBLOCKS, SLOTS, PROJ, BLOCK)
    whole = (QBLOCKS, HEADS, BLOCK, WIDE)
    piece = (HEADS, TILE_COLS, WIDE)
    return pl.pallas_call(
        fused_kernel,
        out_shape=(
            jax.ShapeDtypeStruct(flip, BF),
            jax.ShapeDtypeStruct((PROJ, TILE_ROWS), F32),
            jax.ShapeDtypeStruct((WROWS, PROJ), F32),
        ),
        in_specs=[smem] * 2 + [vmem] * 8,
        out_specs=(vmem, vmem, vmem),
        scratch_shapes=[
            pltpu.VMEM((TILE_ROWS * TILE_COLS, PROJ), F32),
            pltpu.VMEM(flip, BF), pltpu.VMEM(flip, BF),
            pltpu.VMEM(cols, BF), pltpu.VMEM(cols, BF),
            pltpu.VMEM((TILE_ROWS, PROJ), BF), pltpu.VMEM((ROWS, TILE_ROWS, PROJ), BF),
            pltpu.VMEM(piece, BF), pltpu.VMEM(whole, BF),
            pltpu.VMEM((4 * PROJ, PROJ), BF),
            pltpu.VMEM((COL_WIDTH, QBLOCKS, PROJ, HEADS * BLOCK), BF),
            pltpu.VMEM(tiles, BF), pltpu.VMEM(tiles, BF), pltpu.VMEM(tiles, BF),
            pltpu.VMEM(tiles, BF), pltpu.VMEM(tiles, BF),
            pltpu.VMEM(tiles, F32), pltpu.VMEM(tiles, F32),
            pltpu.VMEM(tiles, BF), pltpu.VMEM(tiles, BF), pltpu.VMEM(tiles, BF),
            pltpu.VMEM(slots, F32), pltpu.VMEM(slots, F32),
            pltpu.VMEM((1, WIDE, HEADS * BLOCK), F32),
            pltpu.VMEM((WIDE, HEADS * BLOCK), F32),
            pltpu.VMEM((4 * PROJ, PROJ), F32), pltpu.VMEM((PROJ, PROJ), F32),
            pltpu.VMEM((COL_WIDTH, 4 * PROJ, TOKENS), BF), pltpu.VMEM(cols, BF),
            pltpu.VMEM(whole, BF), pltpu.VMEM((QBLOCKS, 2, *piece), BF),
            pltpu.VMEM((QBLOCKS, 2, *piece), BF), pltpu.VMEM((3, 2, *piece), BF),
            pltpu.VMEM(piece, BF), pltpu.VMEM(piece, BF),
            pltpu.VMEM((TOKENS, PROJ), BF), pltpu.VMEM((7, TILE_ROWS, PROJ), BF),
            pltpu.VMEM((WROWS, PROJ), BF), pltpu.VMEM((7, WPART, PROJ), BF),
            pltpu.VMEM((WPART, PROJ), BF), pltpu.VMEM((COLS, WPART, PROJ), BF),
            dma((N_SEMS,)), dma((N_SEMS,)),
        ],
        compiler_params=pltpu.CompilerParams(
            collective_id=0, has_side_effects=True, vmem_limit_bytes=60 * 1024 * 1024
        ),
        name="attend_back",
    )(key_blocks, list_len, act, grad, bias, *weights)


def on_device(
    pair_act, out_grad, tri_bias, w_query, w_key, w_value, w_gate, w_out, key_blocks, list_len
):
    bias = jnp.transpose(tri_bias, (0, 2, 1)).reshape(PROJ, TILE_ROWS)
    dp, db, ws = fused(
        key_blocks, list_len, pair_act, out_grad, bias, w_query, w_key, w_value, w_gate, w_out
    )
    d_pair = jnp.transpose(dp, (1, 0, 2))
    d_bias = jnp.transpose(db.reshape(HEADS, TILE_COLS, TILE_ROWS), (0, 2, 1))
    return (d_pair, d_bias) + tuple(ws[n * PROJ : (n + 1) * PROJ] for n in range(5))


def solution(mesh):
    in_specs = (
        P("row", "col", None), P("row", "col", None), P(None, "row", "col"),
        P(), P(), P(), P(), P(), P(), P(),
    )
    out_specs = (P("row", "col", None), P(None, "row", "col"), P(), P(), P(), P(), P())
    return jax.shard_map(
        on_device, mesh=mesh, in_specs=in_specs, out_specs=out_specs, check_vma=False
    )
```

```python
import jax
import jax.numpy as jnp
from jax import lax
from jax.experimental import pallas as pl
from jax.experimental.pallas import tpu as pltpu
from jax.sharding import PartitionSpec as P

BF = jnp.bfloat16
F32 = jnp.float32
HEADS = 4
HEAD_DIM = 32
PROJ = HEADS * HEAD_DIM
BLOCK = 128
QBLOCKS = 4
SLOTS = 3
TOKENS = QBLOCKS * BLOCK
WIDE = SLOTS * BLOCK
ROWS = 8
COLS = 16
TILE_ROWS = TOKENS // ROWS
TILE_COLS = TOKENS // COLS
COL_WIDTH = TILE_COLS // ROWS
WROWS = 5 * PROJ
PLANE = 16
PILLAR = 8
WPART = 48
WPAD = WPART * PLANE
DEAD = -1e30
SCALE = HEAD_DIM ** -0.5

ROW_OFFS = [(dz, dx) for dz in range(2) for dx in range(4)][1:]
PLANE_OFFS = [(dz, dx, dh) for dh in range(2) for dz in range(2) for dx in range(4)][1:]
PILLAR_OFFS = [(dy, 0, dc) for dy in range(4) for dc in range(2)][1:]


def row_peer(r, off):
    z, x = r // 4, lax.rem(r, 4)
    return lax.rem(z + off[0], 2) * 4 + lax.rem(x + off[1], 4)


def col_peer(c, off):
    y, z, k = c // 4, lax.rem(c // 2, 2), lax.rem(c, 2)
    return lax.rem(y + off[0], 4) * 4 + lax.rem(z + off[1], 2) * 2 + lax.rem(k + off[2], 2)


def remote(src, dst, ssem, rsem, r, c):
    return pltpu.make_async_remote_copy(
        src_ref=src,
        dst_ref=dst,
        send_sem=ssem,
        recv_sem=rsem,
        device_id=(r, c),
        device_id_type=pl.DeviceIdType.MESH,
    )


NT = (((1,), (1,)), ((), ()))
NN = (((1,), (0,)), ((), ()))


def mm(a, b, dims=NN):
    return lax.dot_general(a, b, dims, preferred_element_type=F32)


def head_rows(x):
    head_of = lax.broadcasted_iota(jnp.int32, x.shape, 0) // HEAD_DIM
    return jnp.concatenate(
        [jnp.where(head_of == h, x, jnp.zeros_like(x)) for h in range(HEADS)], axis=1
    )


def project(act_ref, grad_ref, wk_ref, wv_ref, wo_ref, wt_s, q4_s, qt_s, kt_s, vt_s, k_s, v_s,
            gt_s, dgt_s, w):
    x = act_ref[w]
    turned = mm(wt_s[...], x, NT)
    qt = (turned[:PROJ] * SCALE).astype(BF)
    kt = turned[PROJ : 2 * PROJ].astype(BF)
    vt = turned[2 * PROJ : 3 * PROJ].astype(BF)
    for b in range(QBLOCKS):
        cols = slice(b * BLOCK, (b + 1) * BLOCK)
        qt_s[w, b] = qt[:, cols]
        q4_s[w, b] = head_rows(qt[:, cols])
        kt_s[w, b] = kt[:, cols]
        vt_s[w, b] = vt[:, cols]
        gt_s[w, b] = jax.nn.sigmoid(turned[3 * PROJ :, cols])
    dgt = mm(wo_ref[...], grad_ref[w], NT)
    k = mm(x, wk_ref[...]).astype(BF)
    v = mm(x, wv_ref[...]).astype(BF)
    for b in range(QBLOCKS):
        rows = slice(b * BLOCK, (b + 1) * BLOCK)
        dgt_s[w, b] = dgt[:, rows]
        k_s[w, b] = k[rows]
        v_s[w, b] = v[rows]


def one_pair(kbs, bias_s, q4_s, qt_s, kt_s, vt_s, k_s, v_s, gt_s, dgt_s, dqt_s, dgp_s, gated_s,
             dk_s, dv_s, dacc_s, w, b):
    def chosen(ref, axis):
        return jnp.concatenate([ref[w, kb] for kb in kbs], axis=axis)

    heads = [slice(h * BLOCK, (h + 1) * BLOCK) for h in range(HEADS)]
    scores = mm(chosen(k_s, 0), q4_s[w, b]) + bias_s[b]
    e = jnp.exp(scores - jnp.max(scores, axis=0, keepdims=True))
    e_low = e.astype(BF)
    vt = chosen(vt_s, 1)
    ones = jnp.ones((16, WIDE), BF)
    atts, invs = [], []
    for h in range(0, HEADS, 2):
        lhs = jnp.concatenate([vt[h * HEAD_DIM : (h + 2) * HEAD_DIM], ones], axis=0)
        both = mm(lhs, e_low[:, h * BLOCK : (h + 2) * BLOCK])
        inv = 1.0 / both[2 * HEAD_DIM : 2 * HEAD_DIM + 1]
        for n in range(2):
            part = inv[:, n * BLOCK : (n + 1) * BLOCK]
            raw = both[n * HEAD_DIM : (n + 1) * HEAD_DIM, n * BLOCK : (n + 1) * BLOCK]
            atts.append(raw * part)
            invs.append(jnp.broadcast_to(part, (HEAD_DIM, BLOCK)))
    att = jnp.concatenate(atts, axis=0)
    inv = jnp.concatenate(invs, axis=0)
    g = gt_s[w, b]
    datt = dgt_s[w, b] * g
    gated_s[w, b] = (g * att).astype(BF)
    dgp_s[w, b] = (datt * att * (1.0 - g)).astype(BF)
    dn = (datt * inv).astype(BF)
    prod = dn.astype(F32) * att
    delta = jnp.concatenate(
        [
            jnp.sum(prod[h * HEAD_DIM : (h + 1) * HEAD_DIM], axis=0, keepdims=True)
            for h in range(HEADS)
        ],
        axis=1,
    )
    ds = e * (mm(chosen(v_s, 0), head_rows(dn)) - delta)
    dacc_s[b] += ds
    ds_low = ds.astype(BF)
    kt = chosen(kt_s, 1)
    qt = qt_s[w, b]
    for h in range(HEADS):
        hs = slice(h * HEAD_DIM, (h + 1) * HEAD_DIM)
        dqt_s[w, b, hs, :] = (mm(kt[hs], ds_low[:, heads[h]]) * SCALE).astype(BF)
        dk = mm(qt[hs], ds_low[:, heads[h]], NT)
        dv = mm(dn[hs], e_low[:, heads[h]], NT)
        for s in range(SLOTS):
            dk_s[w, b, s, hs, :] = dk[:, s * BLOCK : (s + 1) * BLOCK]
            dv_s[w, b, s, hs, :] = dv[:, s * BLOCK : (s + 1) * BLOCK]


def collect(kb_ref, len_ref, act_ref, grad_ref, dqt_s, dgp_s, gated_s, dk_s, dv_s, dw_s, dwo_s,
            grads_s, w):
    dks, dvs = [], []
    for k in range(QBLOCKS):
        dk = jnp.zeros((PROJ, BLOCK), F32)
        dv = jnp.zeros((PROJ, BLOCK), F32)
        for b in range(QBLOCKS):
            slot = jnp.int32(SLOTS)
            for s in range(SLOTS):
                slot = jnp.where((kb_ref[b, s] == k) & (s < len_ref[b]), s, slot)
            listed = slot < SLOTS
            at = jnp.minimum(slot, SLOTS - 1)
            dk = dk + jnp.where(listed, dk_s[w, b, at], 0.0)
            dv = dv + jnp.where(listed, dv_s[w, b, at], 0.0)
        dks.append(dk.astype(BF))
        dvs.append(dv.astype(BF))
    parts = [
        jnp.concatenate([dqt_s[w, b] for b in range(QBLOCKS)], axis=1),
        jnp.concatenate(dks, axis=1),
        jnp.concatenate(dvs, axis=1),
        jnp.concatenate([dgp_s[w, b] for b in range(QBLOCKS)], axis=1),
    ]
    grads = jnp.concatenate(parts, axis=0)
    grads_s[w] = grads
    dw_s[...] += mm(grads, act_ref[w])
    gated = jnp.concatenate([gated_s[w, b] for b in range(QBLOCKS)], axis=1)
    dwo_s[...] += mm(gated, grad_ref[w])


class Sems:
    def __init__(self, send, recv):
        self.send, self.recv, self.used = send, recv, 0

    def later(self, src, dst, r, c):
        n = self.used
        self.used += 1
        return remote(src, dst, self.send.at[n], self.recv.at[n], r, c)

    def remote(self, src, dst, r, c):
        cp = self.later(src, dst, r, c)
        cp.start()
        return cp


N_SEMS = 15 + 56 + 6 + 2 + 6 + 28 + 8 + 3 + 15 + 15 + 7 + 15


def fused_kernel(
    kb_ref, len_ref, pair_ref, cot_ref, bias_ref, wq_ref, wk_ref, wv_ref, wg_ref, wo_ref,
    dp_ref, db_ref, wsum_ref,
    flat_s, actt, gradt, act_s, grad_s, turned, got, mine, full,
    wt_s, q4_s, qt_s, kt_s, vt_s, k_s, v_s, gt_s, dgt_s, dqt_s, dgp_s, gated_s, dk_s, dv_s,
    bias_s, dacc_s, dw_s, dwo_s, grads_s, dpair_s,
    part, r1, s1, r2, dense, r4, dwb, r5, s6, w6,
    send_sem, recv_sem,
):
    r, c = lax.axis_index("row"), lax.axis_index("col")
    y, zh, core = c // 4, lax.rem(c // 2, 2), lax.rem(c, 2)
    sems = Sems(send_sem, recv_sem)
    barrier = pltpu.get_barrier_semaphore()
    me, level = zh * 8 + r, y * 2 + core
    plane = []
    for dz, dx, dh in PLANE_OFFS:
        p = row_peer(r, (dz, dx))
        plane.append((lax.rem(zh + dh, 2) * 8 + p, p, col_peer(c, (0, dh, 0))))
    pillar = [col_peer(c, off) for off in PILLAR_OFFS]
    peers = [(p, q) for _, p, q in plane] + [(r, q) for q in pillar]
    for peer in peers:
        pl.semaphore_signal(barrier, inc=1, device_id=peer, device_id_type=pl.DeviceIdType.MESH)

    turned[...] = bias_ref[...].astype(F32).T.astype(BF)
    for src, dst in ((pair_ref, actt), (cot_ref, gradt)):
        flat_s[...] = src[...].astype(F32).reshape(TILE_ROWS * TILE_COLS, PROJ)

        @pl.loop(0, TILE_COLS // 4)
        def _(n):
            for u in range(4):
                j = n * 4 + u
                dst[j] = flat_s[pl.ds(j, TILE_ROWS, stride=TILE_COLS), :].astype(BF)

    got[me] = turned[...]
    pl.semaphore_wait(barrier, len(peers))

    first = [sems.remote(turned, got.at[me], p, q) for _, p, q in plane]
    rows = pl.ds(pl.multiple_of(r * TILE_ROWS, TILE_ROWS), TILE_ROWS)
    big = [[] for _ in range(COL_WIDTH)]

    def spread(w, offs):
        for off in offs:
            p = row_peer(r, off)
            big[w].append(sems.remote(actt.at[p * COL_WIDTH + w], act_s.at[w, rows, :], p, c))
            big[w].append(sems.remote(gradt.at[p * COL_WIDTH + w], grad_s.at[w, rows, :], p, c))

    near = [off for off in ROW_OFFS if off[0] == 0]
    far = [off for off in ROW_OFFS if off[0] == 1]
    for w in range(COL_WIDTH):
        spread(w, far)
        spread(w, near)
    for w in range(COL_WIDTH):
        act_s[w, rows, :] = actt[r * COL_WIDTH + w]
        grad_s[w, rows, :] = gradt[r * COL_WIDTH + w]
    for n, ref in enumerate((wq_ref, wk_ref, wv_ref, wg_ref)):
        wt_s[n * PROJ : (n + 1) * PROJ, :] = ref[...].astype(F32).T.astype(BF)
    dw_s[...] = jnp.zeros_like(dw_s)
    dwo_s[...] = jnp.zeros_like(dwo_s)
    dacc_s[...] = jnp.zeros_like(dacc_s)

    for cp in first:
        cp.wait_recv()
    for z in range(2):
        for s in range(SLOTS):
            k = z * 8 + 2 * kb_ref[y, s]
            tile = jnp.concatenate([got[k], got[k + 1]], axis=0).astype(F32)
            tile = jnp.where(s < len_ref[y], tile, DEAD).T.astype(BF)
            mine[z, :, :, s * BLOCK : (s + 1) * BLOCK] = tile.reshape(HEADS, TILE_COLS, BLOCK)

    def piece(ref, cc):
        at = pl.multiple_of(lax.rem(cc, 4) * TILE_COLS, TILE_COLS)
        return ref.at[cc // 4, :, pl.ds(at, TILE_COLS), :]

    sib = col_peer(c, (0, 0, 1))
    ys = [col_peer(c, (n + 1, 0, 0)) for n in range(3)]

    def layer(cc, z):
        return cc // 4 * 4 + z * 2 + core

    cs = [sems.remote(mine.at[z], piece(full, layer(c, z)), r, sib) for z in range(2)]
    to_y = [None] * 3
    for n in (0, 2, 1):
        to_y[n] = [sems.remote(mine.at[z], piece(full, layer(c, z)), r, ys[n]) for z in range(2)]
    for z in range(2):
        piece(full, layer(c, z))[...] = mine[z]
    fwd = [None] * 3

    def column(w):
        for cp in big[w]:
            cp.wait_recv()
        project(act_s, grad_s, wk_ref, wv_ref, wo_ref, wt_s, q4_s, qt_s, kt_s, vt_s, k_s, v_s,
                gt_s, dgt_s, w)

    def pass_on(n):
        fwd[n] = []
        for z in range(2):
            to_y[n][z].wait_recv()
            cc = layer(col_peer(c, (3 - n, 0, 0)), z)
            fwd[n].append(sems.remote(piece(full, cc), piece(full, cc), r, sib))

    def block_of(t):
        b = lax.rem(y + t, QBLOCKS)
        return b, [kb_ref[b, s] for s in range(SLOTS)]

    def pairs(t, lo, hi, between=None):
        b, kbs = block_of(t)

        @pl.loop(lo, hi)
        def _(w):
            one_pair(kbs, bias_s, q4_s, qt_s, kt_s, vt_s, k_s, v_s, gt_s, dgt_s, dqt_s, dgp_s,
                     gated_s, dk_s, dv_s, dacc_s, w, b)
            if between is not None:
                pl.when(w == lo)(between)

    def bias_block(t):
        b, _ = block_of(t)
        for h in range(HEADS):
            bias_s[b, :, h * BLOCK : (h + 1) * BLOCK] = full[b, h].astype(F32).T

    column(0)
    column(1)
    for cp in cs:
        cp.wait_recv()
    bias_block(0)
    pairs(0, 0, 2)
    pass_on(0)
    column(2)
    pass_on(2)
    for cp in fwd[0]:
        cp.wait_recv()
    bias_block(3)
    pairs(3, 0, 2)
    pass_on(1)
    column(3)
    for t, n in ((1, 2), (2, 1)):
        for cp in fwd[n]:
            cp.wait_recv()
        bias_block(t)
        pairs(t, 0, 2)

    def gather_grads(lo, hi):
        @pl.loop(lo, hi)
        def _(w):
            collect(kb_ref, len_ref, act_s, grad_s, dqt_s, dgp_s, gated_s, dk_s, dv_s, dw_s, dwo_s,
                    grads_s, w)

    cd = []
    w_all = jnp.concatenate([ref[...] for ref in (wq_ref, wk_ref, wv_ref, wg_ref)], axis=1)

    def d_pair(w):
        back = mm(w_all, grads_s[w])
        for b in range(QBLOCKS):
            at = slice(b * BLOCK, (b + 1) * BLOCK)
            dpair_s[w, at, :] = back[:, at].T.astype(BF)

    def give(w, offs):
        for off in offs:
            p = row_peer(r, off)
            src = dpair_s.at[w, pl.ds(pl.multiple_of(p * TILE_ROWS, TILE_ROWS), TILE_ROWS), :]
            cd.append(sems.remote(src, dp_ref.at[r * COL_WIDTH + w], p, c))

    gather_grads(0, 2)
    for w in range(2):
        d_pair(w)
        give(w, far)
        give(w, near)

    c1, c2 = [], []

    def merge(t):
        for n in range(2):
            c1[t][n].wait_recv()
            at = pl.multiple_of((2 * n + core) * TILE_COLS, TILE_COLS)
            own = part[t, :, pl.ds(at, TILE_COLS), :]
            s1[t, n] = (own.astype(F32) + r1[t, n].astype(F32)).astype(BF)

    for t in range(QBLOCKS):
        b, _ = block_of(1 + t)
        if t > 0:
            c2.append(sems.later(s1.at[t - 1], r2.at[t - 1], r, ys[t - 1]))

        def between():
            merge(t - 1)
            c2[t - 1].start()

        pairs(1 + t, 2, COL_WIDTH, between if t > 0 else None)
        for h in range(HEADS):
            part[t, h] = dacc_s[b, :, h * BLOCK : (h + 1) * BLOCK].T.astype(BF)
        now = []
        for n in range(2):
            at = pl.multiple_of((2 * n + 1 - core) * TILE_COLS, TILE_COLS)
            now.append(sems.remote(part.at[t, :, pl.ds(at, TILE_COLS), :], r1.at[t, n], r, sib))
        c1.append(now)

    gather_grads(2, COL_WIDTH)
    for n in range(4):
        at = slice(n * PROJ, (n + 1) * PROJ)
        dwb[at, :] = dw_s[at, :].T.astype(BF)
    dwb[4 * PROJ : WROWS, :] = dwo_s[...].astype(BF)
    dwb[WROWS:, :] = jnp.zeros((WPAD - WROWS, PROJ), BF)
    c5 = []
    for g, p, q in plane:
        src = dwb.at[pl.ds(pl.multiple_of(g * WPART, 16), WPART), :]
        c5.append(sems.remote(src, r5.at[me], p, q))
    myrows = pl.ds(pl.multiple_of(me * WPART, 16), WPART)
    r5[me] = dwb[myrows, :]
    for w in range(2, COL_WIDTH):
        d_pair(w)
        give(w, near)
    merge(3)
    for cp in c2:
        cp.wait_recv()

    for z in range(2):
        acc = s1[3, z].astype(F32)
        for m in range(3):
            acc = acc + r2[m, z].astype(F32)
        tiles = [
            acc[:, :, s * BLOCK : (s + 1) * BLOCK].reshape(PROJ, BLOCK).T for s in range(SLOTS)
        ]
        for k in range(QBLOCKS):
            val = jnp.zeros((BLOCK, PROJ), F32)
            for s in range(SLOTS):
                hit = (kb_ref[y, s] == k) & (s < len_ref[y])
                val = val + jnp.where(hit, tiles[s], 0.0)
            dense[z * QBLOCKS + k] = val.astype(BF)

    def share(g):
        at = pl.multiple_of(lax.rem(g, 2) * TILE_ROWS, TILE_ROWS)
        return dense.at[g // 2, pl.ds(at, TILE_ROWS), :]

    c4 = [sems.remote(share(g), r4.at[me], p, q) for g, p, q in plane]
    r4[me] = share(me)[...]
    for cp in c5:
        cp.wait_recv()
    tot = r5[0].astype(F32)
    for n in range(1, PLANE):
        tot = tot + r5[n].astype(F32)
    s6[...] = tot.astype(BF)
    w6[level] = s6[...]
    c6 = [sems.remote(s6, w6.at[level], r, q) for q in pillar]
    for w in range(2, COL_WIDTH):
        give(w, far)
    for w in range(COL_WIDTH):
        dp_ref[r * COL_WIDTH + w] = dpair_s[w, rows, :]
    for cp in c6:
        cp.wait_recv()
    tot = w6[0].astype(F32)
    for n in range(1, PILLAR):
        tot = tot + w6[n].astype(F32)
    wsum_ref[myrows, :] = tot.astype(BF)
    c7 = [
        sems.remote(wsum_ref.at[myrows, :], wsum_ref.at[myrows, :], p, q) for _, p, q in plane
    ]
    for cp in c4:
        cp.wait_recv()
    val = r4[0].astype(F32)
    for n in range(1, PLANE):
        val = val + r4[n].astype(F32)
    db_ref[...] = val.T
    for cp in cd + c7:
        cp.wait_recv()
    for cp in sum(big + to_y + fwd + c1, []) + first + cs + c2 + c4 + c5 + c6 + c7 + cd:
        cp.wait_send()


def fused(key_blocks, list_len, act, grad, bias, *weights):
    any_ = pl.BlockSpec(memory_space=pl.ANY)
    smem = pl.BlockSpec(memory_space=pltpu.SMEM)
    vmem = pl.BlockSpec(memory_space=pltpu.VMEM)
    dma = pltpu.SemaphoreType.DMA
    flip = (TILE_COLS, TILE_ROWS, PROJ)
    cols = (COL_WIDTH, TOKENS, PROJ)
    tiles = (COL_WIDTH, QBLOCKS, PROJ, BLOCK)
    slots = (COL_WIDTH, QBLOCKS, SLOTS, PROJ, BLOCK)
    whole = (QBLOCKS, HEADS, BLOCK, WIDE)
    piece = (HEADS, TILE_COLS, WIDE)
    return pl.pallas_call(
        fused_kernel,
        out_shape=(
            jax.ShapeDtypeStruct(flip, BF),
            jax.ShapeDtypeStruct((PROJ, TILE_ROWS), F32),
            jax.ShapeDtypeStruct((WPAD, PROJ), BF),
        ),
        in_specs=[smem] * 2 + [vmem] * 8,
        out_specs=(vmem, vmem, vmem),
        scratch_shapes=[
            pltpu.VMEM((TILE_ROWS * TILE_COLS, PROJ), F32),
            pltpu.VMEM(flip, BF), pltpu.VMEM(flip, BF),
            pltpu.VMEM(cols, BF), pltpu.VMEM(cols, BF),
            pltpu.VMEM((TILE_ROWS, PROJ), BF), pltpu.VMEM((PLANE, TILE_ROWS, PROJ), BF),
            pltpu.VMEM((2, *piece), BF), pltpu.VMEM(whole, BF),
            pltpu.VMEM((4 * PROJ, PROJ), BF),
            pltpu.VMEM((COL_WIDTH, QBLOCKS, PROJ, HEADS * BLOCK), BF),
            pltpu.VMEM(tiles, BF), pltpu.VMEM(tiles, BF), pltpu.VMEM(tiles, BF),
            pltpu.VMEM(tiles, BF), pltpu.VMEM(tiles, BF),
            pltpu.VMEM(tiles, F32), pltpu.VMEM(tiles, F32),
            pltpu.VMEM(tiles, BF), pltpu.VMEM(tiles, BF), pltpu.VMEM(tiles, BF),
            pltpu.VMEM(slots, F32), pltpu.VMEM(slots, F32),
            pltpu.VMEM((QBLOCKS, WIDE, HEADS * BLOCK), F32),
            pltpu.VMEM((QBLOCKS, WIDE, HEADS * BLOCK), F32),
            pltpu.VMEM((4 * PROJ, PROJ), F32), pltpu.VMEM((PROJ, PROJ), F32),
            pltpu.VMEM((COL_WIDTH, 4 * PROJ, TOKENS), BF), pltpu.VMEM(cols, BF),
            pltpu.VMEM(whole, BF), pltpu.VMEM((QBLOCKS, 2, *piece), BF),
            pltpu.VMEM((QBLOCKS, 2, *piece), BF), pltpu.VMEM((3, 2, *piece), BF),
            pltpu.VMEM((2 * QBLOCKS, BLOCK, PROJ), BF), pltpu.VMEM((PLANE, TILE_ROWS, PROJ), BF),
            pltpu.VMEM((WPAD, PROJ), BF), pltpu.VMEM((PLANE, WPART, PROJ), BF),
            pltpu.VMEM((WPART, PROJ), BF), pltpu.VMEM((PILLAR, WPART, PROJ), BF),
            dma((N_SEMS,)), dma((N_SEMS,)),
        ],
        compiler_params=pltpu.CompilerParams(
            collective_id=0, has_side_effects=True, vmem_limit_bytes=60 * 1024 * 1024
        ),
        name="attend_back",
    )(key_blocks, list_len, act, grad, bias, *weights)


def on_device(
    pair_act, out_grad, tri_bias, w_query, w_key, w_value, w_gate, w_out, key_blocks, list_len
):
    bias = jnp.transpose(tri_bias, (0, 2, 1)).reshape(PROJ, TILE_ROWS)
    dp, db, ws = fused(
        key_blocks, list_len, pair_act, out_grad, bias, w_query, w_key, w_value, w_gate, w_out
    )
    d_pair = jnp.transpose(dp, (1, 0, 2))
    d_bias = jnp.transpose(db.reshape(HEADS, TILE_COLS, TILE_ROWS), (0, 2, 1))
    return (d_pair, d_bias) + tuple(
        ws[n * PROJ : (n + 1) * PROJ].astype(F32) for n in range(5)
    )


def solution(mesh):
    in_specs = (
        P("row", "col", None), P("row", "col", None), P(None, "row", "col"),
        P(), P(), P(), P(), P(), P(), P(),
    )
    out_specs = (P("row", "col", None), P(None, "row", "col"), P(), P(), P(), P(), P())
    return jax.shard_map(
        on_device, mesh=mesh, in_specs=in_specs, out_specs=out_specs, check_vma=False
    )
```

```python
import functools

import jax
import jax.numpy as jnp
from jax import lax
from jax.experimental import pallas as pl
from jax.experimental.pallas import tpu as pltpu
from jax.sharding import PartitionSpec as P

BF = jnp.bfloat16
F32 = jnp.float32
HEADS = 4
HEAD_DIM = 32
PROJ = HEADS * HEAD_DIM
BLOCK = 128
QBLOCKS = 4
SLOTS = 3
TOKENS = QBLOCKS * BLOCK
WIDE = SLOTS * BLOCK
ROWS = 8
COLS = 16
TILE_ROWS = TOKENS // ROWS
TILE_COLS = TOKENS // COLS
COL_WIDTH = TILE_COLS // ROWS
WROWS = 5 * PROJ
PLANE = 16
PILLAR = 8
WPART = 48
WPAD = WPART * PLANE
DEAD = -1e30
SCALE = HEAD_DIM ** -0.5

ROW_OFFS = [(dz, dx) for dz in range(2) for dx in range(4)][1:]
PLANE_OFFS = [(dz, dx, dh) for dh in range(2) for dz in range(2) for dx in range(4)][1:]
FLAT_OFFS = [(dx, dy) for dx in range(4) for dy in range(4)][1:]
PILLAR_OFFS = [(dz, dh, dc) for dz in range(2) for dh in range(2) for dc in range(2)][1:]


def row_peer(r, off):
    z, x = r // 4, lax.rem(r, 4)
    return lax.rem(z + off[0], 2) * 4 + lax.rem(x + off[1], 4)


def col_peer(c, off):
    y, z, k = c // 4, lax.rem(c // 2, 2), lax.rem(c, 2)
    return lax.rem(y + off[0], 4) * 4 + lax.rem(z + off[1], 2) * 2 + lax.rem(k + off[2], 2)


def remote(src, dst, ssem, rsem, r, c):
    return pltpu.make_async_remote_copy(
        src_ref=src,
        dst_ref=dst,
        send_sem=ssem,
        recv_sem=rsem,
        device_id=(r, c),
        device_id_type=pl.DeviceIdType.MESH,
    )


NT = (((1,), (1,)), ((), ()))
NN = (((1,), (0,)), ((), ()))


def mm(a, b, dims=NN):
    return lax.dot_general(a, b, dims, preferred_element_type=F32)


def head_rows(x):
    head_of = lax.broadcasted_iota(jnp.int32, x.shape, 0) // HEAD_DIM
    return jnp.concatenate(
        [jnp.where(head_of == h, x, jnp.zeros_like(x)) for h in range(HEADS)], axis=1
    )


def head_cols(x):
    head_of = lax.broadcasted_iota(jnp.int32, x.shape, 1) // HEAD_DIM
    return jnp.concatenate(
        [jnp.where(head_of == h, x, jnp.zeros_like(x)) for h in range(HEADS)], axis=0
    )


def project(act_ref, grad_ref, wq_ref, wk_ref, wv_ref, wo_ref, wt_s, q4_s, qn_s, kt_s, vt_s, k_s, v_s,
            gt_s, dgt_s, xt_s, w):
    x = act_ref[w]
    turned = mm(wt_s[...], x, NT)
    qt = (turned[:PROJ] * SCALE).astype(BF)
    kt = turned[PROJ : 2 * PROJ].astype(BF)
    vt = turned[2 * PROJ : 3 * PROJ].astype(BF)
    for b in range(QBLOCKS):
        cols = slice(b * BLOCK, (b + 1) * BLOCK)
        q4_s[w, b] = head_rows(qt[:, cols])
        kt_s[w, b] = kt[:, cols]
        vt_s[w, b] = vt[:, cols]
        gt_s[w, b] = jax.nn.sigmoid(turned[3 * PROJ :, cols])
    dgt = mm(wo_ref[...], grad_ref[w], NT)
    qkv = mm(x, jnp.concatenate([wq_ref[...], wk_ref[...], wv_ref[...]], axis=1))
    q = (qkv[:, :PROJ] * SCALE).astype(BF)
    k = qkv[:, PROJ : 2 * PROJ].astype(BF)
    v = qkv[:, 2 * PROJ :].astype(BF)
    for b in range(QBLOCKS):
        rows = slice(b * BLOCK, (b + 1) * BLOCK)
        dgt_s[w, b] = dgt[:, rows]
        k_s[w, b] = k[rows]
        qn_s[w, b] = head_cols(q[rows])
        xt_s[w, :, rows] = x[rows].astype(F32).T.astype(BF)
        v_s[w, b] = v[rows]


def one_pair(kbs, bias_s, q4_s, qn_s, kt_s, vt_s, k_s, v_s, gt_s, dgt_s, dqt_s, dgp_s, gated_s,
             dk_s, dv_s, dacc_s, w, b):
    def chosen(ref, axis):
        return jnp.concatenate([ref[w, kb] for kb in kbs], axis=axis)

    heads = [slice(h * BLOCK, (h + 1) * BLOCK) for h in range(HEADS)]
    scores = mm(chosen(k_s, 0), q4_s[w, b]) + bias_s[b]
    e = jnp.exp(scores - jnp.max(scores, axis=0, keepdims=True))
    e_low = e.astype(BF)
    vt = chosen(vt_s, 1)
    ones = jnp.ones((16, WIDE), BF)
    atts, invs = [], []
    for h in range(HEADS):
        lhs = jnp.concatenate([vt[h * HEAD_DIM : (h + 1) * HEAD_DIM], ones], axis=0)
        both = mm(lhs, e_low[:, heads[h]])
        part = 1.0 / both[HEAD_DIM : HEAD_DIM + 1]
        atts.append(both[:HEAD_DIM] * part)
        invs.append(jnp.broadcast_to(part, (HEAD_DIM, BLOCK)))
    att = jnp.concatenate(atts, axis=0)
    inv = jnp.concatenate(invs, axis=0)
    g = gt_s[w, b]
    datt = dgt_s[w, b] * g
    gated_s[w, b] = (g * att).astype(BF)
    dgp_s[w, b] = (datt * att * (1.0 - g)).astype(BF)
    dn = (datt * inv).astype(BF)
    prod = dn.astype(F32) * att
    delta = jnp.concatenate(
        [
            jnp.sum(prod[h * HEAD_DIM : (h + 1) * HEAD_DIM], axis=0, keepdims=True)
            for h in range(HEADS)
        ],
        axis=1,
    )
    ds = e * (mm(chosen(v_s, 0), head_rows(dn)) - delta)
    dacc_s[b] += ds
    ds_low = ds.astype(BF)
    kt = chosen(kt_s, 1)
    for h in range(HEADS):
        hs = slice(h * HEAD_DIM, (h + 1) * HEAD_DIM)
        dqt_s[w, b, hs, :] = (mm(kt[hs], ds_low[:, heads[h]]) * SCALE).astype(BF)
    dk = mm(ds_low, qn_s[w, b])
    dv = mm(e_low, head_cols(dn.astype(F32).T.astype(BF)))
    for s in range(SLOTS):
        dk_s[w, b, s] = dk[s * BLOCK : (s + 1) * BLOCK]
        dv_s[w, b, s] = dv[s * BLOCK : (s + 1) * BLOCK]


def collect(kb_ref, len_ref, act_ref, grad_ref, xt_s, dqt_s, dgp_s, gated_s, dk_s, dv_s, dw_s,
            dwkv_s, dwo_s, ga_s, gb_s, w):
    for k in range(QBLOCKS):
        dk = jnp.zeros((BLOCK, PROJ), F32)
        dv = jnp.zeros((BLOCK, PROJ), F32)
        for b in range(QBLOCKS):
            slot = jnp.int32(SLOTS)
            for s in range(SLOTS):
                slot = jnp.where((kb_ref[b, s] == k) & (s < len_ref[b]), s, slot)
            listed = slot < SLOTS
            at = jnp.minimum(slot, SLOTS - 1)
            dk = dk + jnp.where(listed, dk_s[w, b, at], 0.0)
            dv = dv + jnp.where(listed, dv_s[w, b, at], 0.0)
        cols = slice(k * BLOCK, (k + 1) * BLOCK)
        gb_s[w, cols, :PROJ] = dk.astype(BF)
        gb_s[w, cols, PROJ:] = dv.astype(BF)
        ga_s[w, :PROJ, cols] = dqt_s[w, k]
        ga_s[w, PROJ:, cols] = dgp_s[w, k]
    dw_s[...] += mm(ga_s[w], act_ref[w])
    dwkv_s[...] += mm(xt_s[w], gb_s[w])
    gated = jnp.concatenate([gated_s[w, b] for b in range(QBLOCKS)], axis=1)
    dwo_s[...] += mm(gated, grad_ref[w])


(S_BIAS, S_ACT, S_GRAD, S_OWN, S_Y, S_FWD, S_SIB, S_SUM, S_TILE, S_PAIR, S_PART, S_LEVEL, S_LAST) = range(13)
(R_BIAS, R_ACT, R_GRAD, R_OWN, R_Y, R_FWD, R_SIB, R_SUM, R_TILE, R_PAIR, R_PART, R_LEVEL, R_LAST) = (
    0, 1, 5, 9, 10, 13, 16, 20, 23, 24, 28, 29, 30,
)
N_SEND, N_RECV = 13, 31


def settle(ref, sem):
    pltpu.make_async_copy(ref, ref, sem).wait()


def fused_kernel(
    kb_ref, len_ref, pair_ref, cot_ref, bias_ref, wq_ref, wk_ref, wv_ref, wg_ref, wo_ref,
    dp_ref, db_ref, wsum_ref,
    flat_s, actt, gradt, act_s, grad_s, turned, got, mine, full,
    wt_s, q4_s, qn_s, kt_s, vt_s, k_s, v_s, gt_s, dgt_s, dqt_s, dgp_s, gated_s, dk_s, dv_s,
    bias_s, dacc_s, dw_s, dwkv_s, dwo_s, xt_s, ga_s, gb_s, dpair_s, raw, back_s, wtot, local_sem,
    part, r1, s1, r2, dense, r4, dwb, r5, s6, w6,
    send_sem, recv_sem,
):
    r, c = lax.axis_index("row"), lax.axis_index("col")
    y, zh, core = c // 4, lax.rem(c // 2, 2), lax.rem(c, 2)

    def later(src, dst, si, ri, p, q):
        return remote(src, dst, send_sem.at[si], recv_sem.at[ri], p, q)

    def send(*what):
        later(*what).start()

    def arrived(ref, ri):
        settle(ref, recv_sem.at[ri])

    barrier = pltpu.get_barrier_semaphore()
    me, spot, level = zh * 8 + r, y * 4 + lax.rem(r, 4), r // 4 * 4 + zh * 2 + core
    plane = []
    for dz, dx, dh in PLANE_OFFS:
        p = row_peer(r, (dz, dx))
        plane.append((lax.rem(zh + dh, 2) * 8 + p, p, col_peer(c, (0, dh, 0))))
    flat = []
    for dx, dy in FLAT_OFFS:
        p, q = row_peer(r, (0, dx)), col_peer(c, (dy, 0, 0))
        flat.append((q // 4 * 4 + lax.rem(p, 4), p, q))
    pillar = [(row_peer(r, (dz, 0)), col_peer(c, (0, dh, dc))) for dz, dh, dc in PILLAR_OFFS]
    peers = [(p, q) for _, p, q in plane]
    peers += [(p, q) for (_, p, q), off in zip(flat, FLAT_OFFS) if off[1]]
    peers += [peer for peer, off in zip(pillar, PILLAR_OFFS) if off[2]]
    for peer in peers:
        pl.semaphore_signal(barrier, inc=1, device_id=peer, device_id_type=pl.DeviceIdType.MESH)

    loads = [
        pltpu.make_async_copy(src, raw.at[n], local_sem.at[n])
        for n, src in enumerate((pair_ref, cot_ref))
    ]
    for cp in loads:
        cp.start()
    turned[...] = bias_ref[...].astype(F32).T.astype(BF)
    for n, dst in enumerate((actt, gradt)):
        loads[n].wait()
        flat_s[...] = raw[n].astype(F32).reshape(TILE_ROWS * TILE_COLS, PROJ)

        @pl.loop(0, TILE_COLS // 4)
        def _(m):
            for u in range(4):
                j = m * 4 + u
                dst[j] = flat_s[pl.ds(j, TILE_ROWS, stride=TILE_COLS), :].astype(BF)

    got[me] = turned[...]
    pl.semaphore_wait(barrier, len(peers))

    for _, p, q in plane:
        send(turned, got.at[me], S_BIAS, R_BIAS, p, q)
    rows = pl.ds(pl.multiple_of(r * TILE_ROWS, TILE_ROWS), TILE_ROWS)
    def spread(w, offs):
        for off in offs:
            p = row_peer(r, off)
            j = p * COL_WIDTH + w
            send(actt.at[j], act_s.at[w, rows, :], S_ACT, R_ACT + w, p, c)
            send(gradt.at[j], grad_s.at[w, rows, :], S_GRAD, R_GRAD + w, p, c)

    near = [off for off in ROW_OFFS if off[0] == 0]
    far = [off for off in ROW_OFFS if off[0] == 1]
    for w in range(COL_WIDTH):
        spread(w, far)
        spread(w, near)
    for w in range(COL_WIDTH):
        act_s[w, rows, :] = actt[r * COL_WIDTH + w]
        grad_s[w, rows, :] = gradt[r * COL_WIDTH + w]
    for n, ref in enumerate((wq_ref, wk_ref, wv_ref, wg_ref)):
        wt_s[n * PROJ : (n + 1) * PROJ, :] = ref[...].astype(F32).T.astype(BF)
    dw_s[...] = jnp.zeros_like(dw_s)
    dwkv_s[...] = jnp.zeros_like(dwkv_s)
    dwo_s[...] = jnp.zeros_like(dwo_s)
    dacc_s[...] = jnp.zeros_like(dacc_s)

    arrived(got.at[pl.ds(0, PLANE - 1)], R_BIAS)
    for z in range(2):
        for s in range(SLOTS):
            k = z * 8 + 2 * kb_ref[y, s]
            tile = jnp.concatenate([got[k], got[k + 1]], axis=0).astype(F32)
            tile = jnp.where(s < len_ref[y], tile, DEAD).T.astype(BF)
            mine[z, :, :, s * BLOCK : (s + 1) * BLOCK] = tile.reshape(HEADS, TILE_COLS, BLOCK)

    def piece(ref, cc):
        at = pl.multiple_of(lax.rem(cc, 4) * TILE_COLS, TILE_COLS)
        return ref.at[cc // 4, :, pl.ds(at, TILE_COLS), :]

    sib = col_peer(c, (0, 0, 1))
    ys = [col_peer(c, (n + 1, 0, 0)) for n in range(3)]

    def layer(cc, z):
        return cc // 4 * 4 + z * 2 + core

    for z in range(2):
        send(mine.at[z], piece(full, layer(c, z)), S_OWN, R_OWN, r, sib)
    for n in (1, 0, 2):
        for z in range(2):
            send(mine.at[z], piece(full, layer(c, z)), S_Y, R_Y + n, r, ys[n])
    for z in range(2):
        piece(full, layer(c, z))[...] = mine[z]
    def column(w):
        most = pl.ds(0, TOKENS - TILE_ROWS)
        arrived(act_s.at[w, most, :], R_ACT + w)
        arrived(grad_s.at[w, most, :], R_GRAD + w)
        project(act_s, grad_s, wq_ref, wk_ref, wv_ref, wo_ref, wt_s, q4_s, qn_s, kt_s, vt_s, k_s, v_s,
                gt_s, dgt_s, xt_s, w)

    def pass_on(n):
        arrived(mine, R_Y + n)
        for z in range(2):
            cc = layer(col_peer(c, (3 - n, 0, 0)), z)
            send(piece(full, cc), piece(full, cc), S_FWD, R_FWD + n, r, sib)

    def block_of(t):
        b = lax.rem(y + t, QBLOCKS)
        return b, [kb_ref[b, s] for s in range(SLOTS)]

    def pairs(t, lo, hi, between=None):
        b, kbs = block_of(t)

        @pl.loop(lo, hi)
        def _(w):
            one_pair(kbs, bias_s, q4_s, qn_s, kt_s, vt_s, k_s, v_s, gt_s, dgt_s, dqt_s, dgp_s,
                     gated_s, dk_s, dv_s, dacc_s, w, b)
            if between is not None:
                pl.when(w == lo + 1)(between)

    def bias_block(t):
        b, _ = block_of(t)
        for h in range(HEADS):
            bias_s[b, :, h * BLOCK : (h + 1) * BLOCK] = full[b, h].astype(F32).T

    def gather_grads(lo, hi):
        @pl.loop(lo, hi)
        def _(w):
            collect(kb_ref, len_ref, act_s, grad_s, xt_s, dqt_s, dgp_s, gated_s, dk_s, dv_s, dw_s,
                    dwkv_s, dwo_s, ga_s, gb_s, w)

    w_qg = jnp.concatenate([wq_ref[...], wg_ref[...]], axis=1)
    w_kv = jnp.concatenate([wk_ref[...], wv_ref[...]], axis=1)

    def d_pair(w):
        back = mm(w_qg, ga_s[w]) + mm(w_kv, gb_s[w], NT)
        for b in range(QBLOCKS):
            at = slice(b * BLOCK, (b + 1) * BLOCK)
            dpair_s[w, at, :] = back[:, at].T.astype(BF)

    def give(w, offs):
        for off in offs:
            p = row_peer(r, off)
            src = dpair_s.at[w, pl.ds(pl.multiple_of(p * TILE_ROWS, TILE_ROWS), TILE_ROWS), :]
            send(src, back_s.at[r * COL_WIDTH + w], S_PAIR, R_PAIR + w, p, c)

    c2 = [None] * QBLOCKS

    def merge(t):
        arrived(r1.at[t], R_SIB + t)
        for n in range(2):
            at = pl.multiple_of((2 * n + core) * TILE_COLS, TILE_COLS)
            own = part[t, :, pl.ds(at, TILE_COLS), :]
            s1[t, n] = (own.astype(F32) + r1[t, n].astype(F32)).astype(BF)

    def merge_and_send(t):
        merge(t)
        c2[t].start()

    def close_block(t):
        b, _ = block_of(t)
        for h in range(HEADS):
            part[t, h] = dacc_s[b, :, h * BLOCK : (h + 1) * BLOCK].T.astype(BF)
        for n in range(2):
            at = pl.multiple_of((2 * n + 1 - core) * TILE_COLS, TILE_COLS)
            send(part.at[t, :, pl.ds(at, TILE_COLS), :], r1.at[t, n], S_SIB, R_SIB + t, r, sib)
        if t > 0:
            c2[t] = later(s1.at[t], r2.at[t - 1], S_SUM, R_SUM + t - 1, r, ys[t - 1])

    column(0)
    arrived(mine, R_OWN)
    bias_block(0)
    pairs(0, 0, 1)
    column(1)
    pass_on(1)
    pairs(0, 1, 2)
    pass_on(0)
    last = None
    for t, n in ((2, 1), (3, 0), (1, 2)):
        arrived(mine, R_FWD + n)
        bias_block(t)
        if last is None:
            pairs(t, 0, 2)
            column(2)
            column(3)
            pass_on(2)
            pairs(t, 2, COL_WIDTH)
        else:
            pairs(t, 0, COL_WIDTH, functools.partial(merge_and_send, last))
        close_block(t)
        last = t

    gather_grads(0, 2)
    for w in range(2):
        d_pair(w)
        give(w, far)
        give(w, near)
    merge_and_send(last)
    pairs(0, 2, 3)
    gather_grads(2, 3)
    d_pair(2)
    give(2, far)
    give(2, near)
    pairs(0, 3, COL_WIDTH)
    close_block(0)
    gather_grads(3, COL_WIDTH)
    dwb[:PROJ, :] = dw_s[:PROJ, :].T.astype(BF)
    dwb[PROJ : 2 * PROJ, :] = dwkv_s[:, :PROJ].astype(BF)
    dwb[2 * PROJ : 3 * PROJ, :] = dwkv_s[:, PROJ:].astype(BF)
    dwb[3 * PROJ : 4 * PROJ, :] = dw_s[PROJ:, :].T.astype(BF)
    dwb[4 * PROJ : WROWS, :] = dwo_s[...].astype(BF)
    dwb[WROWS:, :] = jnp.zeros((WPAD - WROWS, PROJ), BF)
    for g, p, q in flat:
        src = dwb.at[pl.ds(pl.multiple_of(g * WPART, 16), WPART), :]
        send(src, r5.at[spot], S_PART, R_PART, p, q)
    myrows = pl.ds(pl.multiple_of(spot * WPART, 16), WPART)
    r5[spot] = dwb[myrows, :]
    d_pair(3)
    arrived(r5.at[pl.ds(0, PLANE - 1)], R_PART)
    tot = r5[0].astype(F32)
    for n in range(1, PLANE):
        tot = tot + r5[n].astype(F32)
    s6[...] = tot.astype(BF)
    w6[level] = s6[...]
    for p, q in pillar:
        send(s6, w6.at[level], S_LEVEL, R_LEVEL, p, q)
    merge(0)
    for n in range(3):
        arrived(r2.at[n], R_SUM + n)

    for z in range(2):
        acc = s1[0, z].astype(F32)
        for m in range(3):
            acc = acc + r2[m, z].astype(F32)
        tiles = [
            acc[:, :, s * BLOCK : (s + 1) * BLOCK].reshape(PROJ, BLOCK).T for s in range(SLOTS)
        ]
        for k in range(QBLOCKS):
            val = jnp.zeros((BLOCK, PROJ), F32)
            for s in range(SLOTS):
                hit = (kb_ref[y, s] == k) & (s < len_ref[y])
                val = val + jnp.where(hit, tiles[s], 0.0)
            dense[z * QBLOCKS + k] = val.astype(BF)

    def share(g):
        at = pl.multiple_of(lax.rem(g, 2) * TILE_ROWS, TILE_ROWS)
        return dense.at[g // 2, pl.ds(at, TILE_ROWS), :]

    r4[me] = share(me)[...]
    for g, p, q in plane:
        send(share(g), r4.at[me], S_TILE, R_TILE, p, q)
    give(3, far)
    give(3, near)
    def turn_back(w):
        arrived(back_s.at[pl.ds(0, ROWS - 1)], R_PAIR + w)
        back_s[r * COL_WIDTH + w] = dpair_s[w, rows, :]

        @pl.loop(0, ROWS)
        def _(n):
            j = n * COL_WIDTH + w
            flat_s[pl.ds(j, TILE_ROWS, stride=TILE_COLS), :] = back_s[j].astype(F32)

    stay = []
    for w in range(3):
        turn_back(w)
    arrived(w6.at[pl.ds(0, PILLAR - 1)], R_LEVEL)
    tot = w6[0].astype(F32)
    for n in range(1, PILLAR):
        tot = tot + w6[n].astype(F32)
    wtot[...] = tot.astype(BF)
    stay.append(pltpu.make_async_copy(wtot, wsum_ref.at[myrows, :], local_sem.at[2]))
    stay[-1].start()
    for _, p, q in flat:
        send(wtot, wsum_ref.at[myrows, :], S_LAST, R_LAST, p, q)
    arrived(r4.at[pl.ds(0, PLANE - 1)], R_TILE)
    val = r4[0].astype(F32)
    for n in range(1, PLANE):
        val = val + r4[n].astype(F32)
    db_ref[...] = val.T
    turn_back(3)
    dp_ref[...] = flat_s[...].reshape(TILE_ROWS, TILE_COLS, PROJ).astype(BF)
    arrived(r5.at[pl.ds(0, PLANE - 1)], R_LAST)
    for cp in stay:
        cp.wait()
    for ref, n in (
        (got.at[pl.ds(0, PLANE - 1)], S_BIAS),
        (actt.at[pl.ds(0, 28)], S_ACT),
        (gradt.at[pl.ds(0, 28)], S_GRAD),
        (mine, S_OWN),
        (r2, S_Y),
        (r2, S_FWD),
        (r1, S_SIB),
        (r2, S_SUM),
        (r4.at[pl.ds(0, PLANE - 1)], S_TILE),
        (back_s.at[pl.ds(0, 28)], S_PAIR),
        (r5.at[pl.ds(0, PLANE - 1)], S_PART),
        (w6.at[pl.ds(0, PILLAR - 1)], S_LEVEL),
        (r5.at[pl.ds(0, PLANE - 1)], S_LAST),
    ):
        settle(ref, send_sem.at[n])


def fused(key_blocks, list_len, act, grad, bias, *weights):
    any_ = pl.BlockSpec(memory_space=pl.ANY)
    smem = pl.BlockSpec(memory_space=pltpu.SMEM)
    vmem = pl.BlockSpec(memory_space=pltpu.VMEM)
    dma = pltpu.SemaphoreType.DMA
    flip = (TILE_COLS, TILE_ROWS, PROJ)
    cols = (COL_WIDTH, TOKENS, PROJ)
    tiles = (COL_WIDTH, QBLOCKS, PROJ, BLOCK)
    slots = (COL_WIDTH, QBLOCKS, SLOTS, PROJ, BLOCK)
    whole = (QBLOCKS, HEADS, BLOCK, WIDE)
    piece = (HEADS, TILE_COLS, WIDE)
    return pl.pallas_call(
        fused_kernel,
        out_shape=(
            jax.ShapeDtypeStruct((TILE_ROWS, TILE_COLS, PROJ), BF),
            jax.ShapeDtypeStruct((PROJ, TILE_ROWS), F32),
            jax.ShapeDtypeStruct((WPAD, PROJ), BF),
        ),
        in_specs=[smem] * 2 + [any_] * 2 + [vmem] * 6,
        out_specs=(vmem, vmem, any_),
        scratch_shapes=[
            pltpu.VMEM((TILE_ROWS * TILE_COLS, PROJ), F32),
            pltpu.VMEM(flip, BF), pltpu.VMEM(flip, BF),
            pltpu.VMEM(cols, BF), pltpu.VMEM(cols, BF),
            pltpu.VMEM((TILE_ROWS, PROJ), BF), pltpu.VMEM((PLANE, TILE_ROWS, PROJ), BF),
            pltpu.VMEM((2, *piece), BF), pltpu.VMEM(whole, BF),
            pltpu.VMEM((4 * PROJ, PROJ), BF),
            pltpu.VMEM((COL_WIDTH, QBLOCKS, PROJ, HEADS * BLOCK), BF),
            pltpu.VMEM((COL_WIDTH, QBLOCKS, HEADS * BLOCK, PROJ), BF),
            pltpu.VMEM(tiles, BF), pltpu.VMEM(tiles, BF),
            pltpu.VMEM(tiles, BF), pltpu.VMEM(tiles, BF),
            pltpu.VMEM(tiles, F32), pltpu.VMEM(tiles, F32),
            pltpu.VMEM(tiles, BF), pltpu.VMEM(tiles, BF), pltpu.VMEM(tiles, BF),
            pltpu.VMEM(slots, F32), pltpu.VMEM(slots, F32),
            pltpu.VMEM((QBLOCKS, WIDE, HEADS * BLOCK), F32),
            pltpu.VMEM((QBLOCKS, WIDE, HEADS * BLOCK), F32),
            pltpu.VMEM((2 * PROJ, PROJ), F32), pltpu.VMEM((PROJ, 2 * PROJ), F32),
            pltpu.VMEM((PROJ, PROJ), F32), pltpu.VMEM((COL_WIDTH, PROJ, TOKENS), BF),
            pltpu.VMEM((COL_WIDTH, 2 * PROJ, TOKENS), BF),
            pltpu.VMEM((COL_WIDTH, TOKENS, 2 * PROJ), BF), pltpu.VMEM(cols, BF),
            pltpu.VMEM((2, TILE_ROWS, TILE_COLS, PROJ), BF), pltpu.VMEM(flip, BF),
            pltpu.VMEM((WPART, PROJ), BF), dma((3,)),
            pltpu.VMEM(whole, BF), pltpu.VMEM((QBLOCKS, 2, *piece), BF),
            pltpu.VMEM((QBLOCKS, 2, *piece), BF), pltpu.VMEM((3, 2, *piece), BF),
            pltpu.VMEM((2 * QBLOCKS, BLOCK, PROJ), BF), pltpu.VMEM((PLANE, TILE_ROWS, PROJ), BF),
            pltpu.VMEM((WPAD, PROJ), BF), pltpu.VMEM((PLANE, WPART, PROJ), BF),
            pltpu.VMEM((WPART, PROJ), BF), pltpu.VMEM((PILLAR, WPART, PROJ), BF),
            dma((N_SEND,)), dma((N_RECV,)),
        ],
        compiler_params=pltpu.CompilerParams(
            collective_id=0, has_side_effects=True, vmem_limit_bytes=60 * 1024 * 1024
        ),
        name="attend_back",
    )(key_blocks, list_len, act, grad, bias, *weights)


def on_device(
    pair_act, out_grad, tri_bias, w_query, w_key, w_value, w_gate, w_out, key_blocks, list_len
):
    bias = jnp.transpose(tri_bias, (0, 2, 1)).reshape(PROJ, TILE_ROWS)
    dp, db, ws = fused(
        key_blocks, list_len, pair_act, out_grad, bias, w_query, w_key, w_value, w_gate, w_out
    )
    d_bias = jnp.transpose(db.reshape(HEADS, TILE_COLS, TILE_ROWS), (0, 2, 1))
    return (dp, d_bias) + tuple(
        ws[n * PROJ : (n + 1) * PROJ].astype(F32) for n in range(5)
    )


def solution(mesh):
    in_specs = (
        P("row", "col", None), P("row", "col", None), P(None, "row", "col"),
        P(), P(), P(), P(), P(), P(), P(),
    )
    out_specs = (P("row", "col", None), P(None, "row", "col"), P(), P(), P(), P(), P())
    return jax.shard_map(
        on_device, mesh=mesh, in_specs=in_specs, out_specs=out_specs, check_vma=False
    )
```

```python
import functools

import jax
import jax.numpy as jnp
from jax import lax
from jax.experimental import pallas as pl
from jax.experimental.pallas import tpu as pltpu
from jax.sharding import PartitionSpec as P

BF = jnp.bfloat16
F32 = jnp.float32
HEADS = 4
HEAD_DIM = 32
PROJ = HEADS * HEAD_DIM
BLOCK = 128
QBLOCKS = 4
SLOTS = 3
TOKENS = QBLOCKS * BLOCK
WIDE = SLOTS * BLOCK
ROWS = 8
COLS = 16
TILE_ROWS = TOKENS // ROWS
TILE_COLS = TOKENS // COLS
COL_WIDTH = TILE_COLS // ROWS
WROWS = 5 * PROJ
PLANE = 16
PILLAR = 8
WPART = 48
WPAD = WPART * PLANE
DEAD = -1e30
SCALE = HEAD_DIM ** -0.5

ROW_OFFS = [(dz, dx) for dz in range(2) for dx in range(4)][1:]
PLANE_OFFS = [(dz, dx, dh) for dh in range(2) for dz in range(2) for dx in range(4)][1:]
FLAT_OFFS = [(dx, dy) for dx in range(4) for dy in range(4)][1:]
PILLAR_OFFS = [(dz, dh, dc) for dz in range(2) for dh in range(2) for dc in range(2)][1:]


def row_peer(r, off):
    z, x = r // 4, lax.rem(r, 4)
    return lax.rem(z + off[0], 2) * 4 + lax.rem(x + off[1], 4)


def col_peer(c, off):
    y, z, k = c // 4, lax.rem(c // 2, 2), lax.rem(c, 2)
    return lax.rem(y + off[0], 4) * 4 + lax.rem(z + off[1], 2) * 2 + lax.rem(k + off[2], 2)


def remote(src, dst, ssem, rsem, r, c):
    return pltpu.make_async_remote_copy(
        src_ref=src,
        dst_ref=dst,
        send_sem=ssem,
        recv_sem=rsem,
        device_id=(r, c),
        device_id_type=pl.DeviceIdType.MESH,
    )


NT = (((1,), (1,)), ((), ()))
NN = (((1,), (0,)), ((), ()))


def mm(a, b, dims=NN):
    return lax.dot_general(a, b, dims, preferred_element_type=F32)


def head_rows(x):
    head_of = lax.broadcasted_iota(jnp.int32, x.shape, 0) // HEAD_DIM
    return jnp.concatenate(
        [jnp.where(head_of == h, x, jnp.zeros_like(x)) for h in range(HEADS)], axis=1
    )


def head_cols(x):
    head_of = lax.broadcasted_iota(jnp.int32, x.shape, 1) // HEAD_DIM
    return jnp.concatenate(
        [jnp.where(head_of == h, x, jnp.zeros_like(x)) for h in range(HEADS)], axis=0
    )


def project(act_ref, grad_ref, wq_ref, wk_ref, wv_ref, wo_ref, wt_s, q4_s, qn_s, kt_s, vt_s, k_s, v_s,
            gt_s, dgt_s, xt_s, w):
    x = act_ref[w]
    turned = mm(wt_s[...], x, NT)
    qt = (turned[:PROJ] * SCALE).astype(BF)
    kt = turned[PROJ : 2 * PROJ].astype(BF)
    vt = turned[2 * PROJ : 3 * PROJ].astype(BF)
    for b in range(QBLOCKS):
        cols = slice(b * BLOCK, (b + 1) * BLOCK)
        q4_s[w, b] = head_rows(qt[:, cols])
        kt_s[w, b] = kt[:, cols]
        vt_s[w, b] = vt[:, cols]
        gt_s[w, b] = jax.nn.sigmoid(turned[3 * PROJ :, cols])
    dgt = mm(wo_ref[...], grad_ref[w], NT)
    qkv = mm(x, jnp.concatenate([wq_ref[...], wk_ref[...], wv_ref[...]], axis=1))
    q = (qkv[:, :PROJ] * SCALE).astype(BF)
    k = qkv[:, PROJ : 2 * PROJ].astype(BF)
    v = qkv[:, 2 * PROJ :].astype(BF)
    for b in range(QBLOCKS):
        rows = slice(b * BLOCK, (b + 1) * BLOCK)
        dgt_s[w, b] = dgt[:, rows]
        k_s[w, b] = k[rows]
        qn_s[w, b] = head_cols(q[rows])
        xt_s[w, :, rows] = x[rows].astype(F32).T.astype(BF)
        v_s[w, b] = v[rows]


def one_pair(kbs, bias_s, q4_s, qn_s, kt_s, vt_s, k_s, v_s, gt_s, dgt_s, dqt_s, dgp_s, gated_s,
             dk_s, dv_s, dacc_s, w, b):
    def chosen(ref, axis):
        return jnp.concatenate([ref[w, kb] for kb in kbs], axis=axis)

    heads = [slice(h * BLOCK, (h + 1) * BLOCK) for h in range(HEADS)]
    scores = mm(chosen(k_s, 0), q4_s[w, b]) + bias_s[b]
    e = jnp.exp(scores - jnp.max(scores, axis=0, keepdims=True))
    e_low = e.astype(BF)
    vt = chosen(vt_s, 1)
    ones = jnp.ones((16, WIDE), BF)
    atts, invs = [], []
    for h in range(HEADS):
        lhs = jnp.concatenate([vt[h * HEAD_DIM : (h + 1) * HEAD_DIM], ones], axis=0)
        both = mm(lhs, e_low[:, heads[h]])
        part = 1.0 / both[HEAD_DIM : HEAD_DIM + 1]
        atts.append(both[:HEAD_DIM] * part)
        invs.append(jnp.broadcast_to(part, (HEAD_DIM, BLOCK)))
    att = jnp.concatenate(atts, axis=0)
    inv = jnp.concatenate(invs, axis=0)
    g = gt_s[w, b]
    datt = dgt_s[w, b] * g
    gated_s[w, b] = (g * att).astype(BF)
    dgp_s[w, b] = (datt * att * (1.0 - g)).astype(BF)
    dn = (datt * inv).astype(BF)
    prod = dn.astype(F32) * att
    delta = jnp.concatenate(
        [
            jnp.sum(prod[h * HEAD_DIM : (h + 1) * HEAD_DIM], axis=0, keepdims=True)
            for h in range(HEADS)
        ],
        axis=1,
    )
    ds = e * (mm(chosen(v_s, 0), head_rows(dn)) - delta)
    dacc_s[b] += ds
    ds_low = ds.astype(BF)
    kt = chosen(kt_s, 1)
    for h in range(HEADS):
        hs = slice(h * HEAD_DIM, (h + 1) * HEAD_DIM)
        dqt_s[w, b, hs, :] = (mm(kt[hs], ds_low[:, heads[h]]) * SCALE).astype(BF)
    dk = mm(ds_low, qn_s[w, b])
    dv = mm(e_low, head_cols(dn.astype(F32).T.astype(BF)))
    for s in range(SLOTS):
        dk_s[w, b, s] = dk[s * BLOCK : (s + 1) * BLOCK]
        dv_s[w, b, s] = dv[s * BLOCK : (s + 1) * BLOCK]


def collect(kb_ref, len_ref, act_ref, grad_ref, xt_s, dqt_s, dgp_s, gated_s, dk_s, dv_s, dw_s,
            dwkv_s, dwo_s, ga_s, gb_s, w):
    for k in range(QBLOCKS):
        dk = jnp.zeros((BLOCK, PROJ), F32)
        dv = jnp.zeros((BLOCK, PROJ), F32)
        for b in range(QBLOCKS):
            slot = jnp.int32(SLOTS)
            for s in range(SLOTS):
                slot = jnp.where((kb_ref[b, s] == k) & (s < len_ref[b]), s, slot)
            listed = slot < SLOTS
            at = jnp.minimum(slot, SLOTS - 1)
            dk = dk + jnp.where(listed, dk_s[w, b, at], 0.0)
            dv = dv + jnp.where(listed, dv_s[w, b, at], 0.0)
        cols = slice(k * BLOCK, (k + 1) * BLOCK)
        gb_s[w, cols, :PROJ] = dk.astype(BF)
        gb_s[w, cols, PROJ:] = dv.astype(BF)
        ga_s[w, :PROJ, cols] = dqt_s[w, k]
        ga_s[w, PROJ:, cols] = dgp_s[w, k]
    dw_s[...] += mm(ga_s[w], act_ref[w])
    dwkv_s[...] += mm(xt_s[w], gb_s[w])
    gated = jnp.concatenate([gated_s[w, b] for b in range(QBLOCKS)], axis=1)
    dwo_s[...] += mm(gated, grad_ref[w])


(S_BIAS, S_ACT, S_GRAD, S_OWN, S_Y, S_FWD, S_SIB, S_SUM, S_TILE, S_PAIR, S_PART, S_LEVEL, S_LAST) = range(13)
(R_BIAS, R_ACT, R_GRAD, R_OWN, R_Y, R_FWD, R_SIB, R_SUM, R_TILE, R_PAIR, R_PART, R_LEVEL, R_LAST) = (
    0, 1, 5, 9, 10, 13, 16, 20, 23, 24, 28, 29, 30,
)
R_FAR = 31
N_SEND, N_RECV = 13, 32


def settle(ref, sem):
    pltpu.make_async_copy(ref, ref, sem).wait()


def fused_kernel(
    kb_ref, len_ref, pair_ref, cot_ref, bias_ref, wq_ref, wk_ref, wv_ref, wg_ref, wo_ref,
    dp_ref, db_ref, wsum_ref,
    flat_s, actt, gradt, act_s, grad_s, turned, near_s, far_s, mine, full,
    wt_s, q4_s, qn_s, kt_s, vt_s, k_s, v_s, gt_s, dgt_s, dqt_s, dgp_s, gated_s, dk_s, dv_s,
    bias_s, dacc_s, dw_s, dwkv_s, dwo_s, xt_s, ga_s, gb_s, dpair_s, raw, back_s, wtot, local_sem,
    part, r1, s1, r2, dense, r4, dwb, r5, s6, w6,
    send_sem, recv_sem,
):
    r, c = lax.axis_index("row"), lax.axis_index("col")
    y, zh, core = c // 4, lax.rem(c // 2, 2), lax.rem(c, 2)

    def later(src, dst, si, ri, p, q):
        return remote(src, dst, send_sem.at[si], recv_sem.at[ri], p, q)

    def send(*what):
        later(*what).start()

    def arrived(ref, ri):
        settle(ref, recv_sem.at[ri])

    barrier = pltpu.get_barrier_semaphore()
    me, spot, level = zh * 8 + r, y * 4 + lax.rem(r, 4), r // 4 * 4 + zh * 2 + core
    plane = []
    for dz, dx, dh in PLANE_OFFS:
        p = row_peer(r, (dz, dx))
        plane.append((lax.rem(zh + dh, 2) * 8 + p, p, col_peer(c, (0, dh, 0))))
    flat = []
    for dx, dy in FLAT_OFFS:
        p, q = row_peer(r, (0, dx)), col_peer(c, (dy, 0, 0))
        flat.append((q // 4 * 4 + lax.rem(p, 4), p, q))
    pillar = [(row_peer(r, (dz, 0)), col_peer(c, (0, dh, dc))) for dz, dh, dc in PILLAR_OFFS]
    peers = [(p, q) for _, p, q in plane]
    peers += [(p, q) for (_, p, q), off in zip(flat, FLAT_OFFS) if off[1]]
    peers += [peer for peer, off in zip(pillar, PILLAR_OFFS) if off[2]]
    for peer in peers:
        pl.semaphore_signal(barrier, inc=1, device_id=peer, device_id_type=pl.DeviceIdType.MESH)

    loads = [
        pltpu.make_async_copy(src, raw.at[n], local_sem.at[n])
        for n, src in enumerate((pair_ref, cot_ref))
    ]
    for cp in loads:
        cp.start()
    turned[...] = bias_ref[...].astype(F32).T.astype(BF)
    for n, dst in enumerate((actt, gradt)):
        loads[n].wait()
        flat_s[...] = raw[n].astype(F32).reshape(TILE_ROWS * TILE_COLS, PROJ)

        @pl.loop(0, TILE_COLS // 4)
        def _(m):
            for u in range(4):
                j = m * 4 + u
                dst[j] = flat_s[pl.ds(j, TILE_ROWS, stride=TILE_COLS), :].astype(BF)

    near_s[r] = turned[...]
    pl.semaphore_wait(barrier, len(peers))

    for n, (_, p, q) in enumerate(plane):
        dst, ri = (near_s, R_BIAS) if n < ROWS - 1 else (far_s, R_FAR)
        send(turned, dst.at[r], S_BIAS, ri, p, q)
    rows = pl.ds(pl.multiple_of(r * TILE_ROWS, TILE_ROWS), TILE_ROWS)
    def spread(w, offs):
        for off in offs:
            p = row_peer(r, off)
            j = p * COL_WIDTH + w
            send(actt.at[j], act_s.at[w, rows, :], S_ACT, R_ACT + w, p, c)
            send(gradt.at[j], grad_s.at[w, rows, :], S_GRAD, R_GRAD + w, p, c)

    near = [off for off in ROW_OFFS if off[0] == 0]
    far = [off for off in ROW_OFFS if off[0] == 1]
    for w in range(COL_WIDTH):
        spread(w, far)
        spread(w, near)
    for w in range(COL_WIDTH):
        act_s[w, rows, :] = actt[r * COL_WIDTH + w]
        grad_s[w, rows, :] = gradt[r * COL_WIDTH + w]
    for n, ref in enumerate((wq_ref, wk_ref, wv_ref, wg_ref)):
        wt_s[n * PROJ : (n + 1) * PROJ, :] = ref[...].astype(F32).T.astype(BF)
    dw_s[...] = jnp.zeros_like(dw_s)
    dwkv_s[...] = jnp.zeros_like(dwkv_s)
    dwo_s[...] = jnp.zeros_like(dwo_s)
    dacc_s[...] = jnp.zeros_like(dacc_s)

    def piece(ref, cc):
        at = pl.multiple_of(lax.rem(cc, 4) * TILE_COLS, TILE_COLS)
        return ref.at[cc // 4, :, pl.ds(at, TILE_COLS), :]

    sib = col_peer(c, (0, 0, 1))
    ys = [col_peer(c, (n + 1, 0, 0)) for n in range(3)]

    def layer(cc, z):
        return cc // 4 * 4 + z * 2 + core

    for first in range(2):
        z, got = (1 - zh, far_s) if first else (zh, near_s)
        arrived(got.at[pl.ds(0, ROWS - 1 + first)], R_FAR if first else R_BIAS)
        for s in range(SLOTS):
            k = 2 * kb_ref[y, s]
            tile = jnp.concatenate([got[k], got[k + 1]], axis=0).astype(F32)
            tile = jnp.where(s < len_ref[y], tile, DEAD).T.astype(BF)
            mine[z, :, :, s * BLOCK : (s + 1) * BLOCK] = tile.reshape(HEADS, TILE_COLS, BLOCK)
        send(mine.at[z], piece(full, layer(c, z)), S_OWN, R_OWN, r, sib)
        for n in (1, 0, 2):
            send(mine.at[z], piece(full, layer(c, z)), S_Y, R_Y + n, r, ys[n])
        piece(full, layer(c, z))[...] = mine[z]

    def column(w):
        most = pl.ds(0, TOKENS - TILE_ROWS)
        arrived(act_s.at[w, most, :], R_ACT + w)
        arrived(grad_s.at[w, most, :], R_GRAD + w)
        project(act_s, grad_s, wq_ref, wk_ref, wv_ref, wo_ref, wt_s, q4_s, qn_s, kt_s, vt_s, k_s, v_s,
                gt_s, dgt_s, xt_s, w)

    def pass_on(n):
        arrived(mine, R_Y + n)
        for z in range(2):
            cc = layer(col_peer(c, (3 - n, 0, 0)), z)
            send(piece(full, cc), piece(full, cc), S_FWD, R_FWD + n, r, sib)

    def block_of(t):
        b = lax.rem(y + t, QBLOCKS)
        return b, [kb_ref[b, s] for s in range(SLOTS)]

    def pairs(t, lo, hi, between=None):
        b, kbs = block_of(t)

        @pl.loop(lo, hi)
        def _(w):
            one_pair(kbs, bias_s, q4_s, qn_s, kt_s, vt_s, k_s, v_s, gt_s, dgt_s, dqt_s, dgp_s,
                     gated_s, dk_s, dv_s, dacc_s, w, b)
            if between is not None:
                pl.when(w == lo + 1)(between)

    def bias_block(t):
        b, _ = block_of(t)
        for h in range(HEADS):
            bias_s[b, :, h * BLOCK : (h + 1) * BLOCK] = full[b, h].astype(F32).T

    def gather_grads(lo, hi):
        @pl.loop(lo, hi)
        def _(w):
            collect(kb_ref, len_ref, act_s, grad_s, xt_s, dqt_s, dgp_s, gated_s, dk_s, dv_s, dw_s,
                    dwkv_s, dwo_s, ga_s, gb_s, w)

    w_qg = jnp.concatenate([wq_ref[...], wg_ref[...]], axis=1)
    w_kv = jnp.concatenate([wk_ref[...], wv_ref[...]], axis=1)

    def d_pair(w):
        back = mm(w_qg, ga_s[w]) + mm(w_kv, gb_s[w], NT)
        for b in range(QBLOCKS):
            at = slice(b * BLOCK, (b + 1) * BLOCK)
            dpair_s[w, at, :] = back[:, at].T.astype(BF)

    def give(w, offs):
        for off in offs:
            p = row_peer(r, off)
            src = dpair_s.at[w, pl.ds(pl.multiple_of(p * TILE_ROWS, TILE_ROWS), TILE_ROWS), :]
            send(src, back_s.at[r * COL_WIDTH + w], S_PAIR, R_PAIR + w, p, c)

    c2 = [None] * QBLOCKS

    def merge(t):
        arrived(r1.at[t], R_SIB + t)
        for n in range(2):
            at = pl.multiple_of((2 * n + core) * TILE_COLS, TILE_COLS)
            own = part[t, :, pl.ds(at, TILE_COLS), :]
            s1[t, n] = (own.astype(F32) + r1[t, n].astype(F32)).astype(BF)

    def merge_and_send(t):
        merge(t)
        c2[t].start()

    def close_block(t):
        b, _ = block_of(t)
        for h in range(HEADS):
            part[t, h] = dacc_s[b, :, h * BLOCK : (h + 1) * BLOCK].T.astype(BF)
        for n in range(2):
            at = pl.multiple_of((2 * n + 1 - core) * TILE_COLS, TILE_COLS)
            send(part.at[t, :, pl.ds(at, TILE_COLS), :], r1.at[t, n], S_SIB, R_SIB + t, r, sib)
        if t > 0:
            c2[t] = later(s1.at[t], r2.at[t - 1], S_SUM, R_SUM + t - 1, r, ys[t - 1])

    column(0)
    arrived(mine, R_OWN)
    bias_block(0)
    pairs(0, 0, 1)
    column(1)
    pass_on(1)
    pairs(0, 1, 2)
    pass_on(0)
    last = None
    for t, n in ((2, 1), (3, 0), (1, 2)):
        arrived(mine, R_FWD + n)
        bias_block(t)
        if last is None:
            pairs(t, 0, 2)
            column(2)
            column(3)
            pass_on(2)
            pairs(t, 2, COL_WIDTH)
        else:
            pairs(t, 0, COL_WIDTH, functools.partial(merge_and_send, last))
        close_block(t)
        last = t

    gather_grads(0, 2)
    for w in range(2):
        d_pair(w)
        give(w, far)
        give(w, near)
    merge_and_send(last)
    pairs(0, 2, 3)
    gather_grads(2, 3)
    pairs(0, 3, COL_WIDTH)
    gather_grads(3, COL_WIDTH)
    dwb[:PROJ, :] = dw_s[:PROJ, :].T.astype(BF)
    dwb[PROJ : 2 * PROJ, :] = dwkv_s[:, :PROJ].astype(BF)
    dwb[2 * PROJ : 3 * PROJ, :] = dwkv_s[:, PROJ:].astype(BF)
    dwb[3 * PROJ : 4 * PROJ, :] = dw_s[PROJ:, :].T.astype(BF)
    dwb[4 * PROJ : WROWS, :] = dwo_s[...].astype(BF)
    dwb[WROWS:, :] = jnp.zeros((WPAD - WROWS, PROJ), BF)
    for g, p, q in flat:
        src = dwb.at[pl.ds(pl.multiple_of(g * WPART, 16), WPART), :]
        send(src, r5.at[spot], S_PART, R_PART, p, q)
    myrows = pl.ds(pl.multiple_of(spot * WPART, 16), WPART)
    r5[spot] = dwb[myrows, :]
    close_block(0)
    for w in range(2, COL_WIDTH):
        d_pair(w)
        give(w, far)
        give(w, near)
    arrived(r5.at[pl.ds(0, PLANE - 1)], R_PART)
    tot = r5[0].astype(F32)
    for n in range(1, PLANE):
        tot = tot + r5[n].astype(F32)
    s6[...] = tot.astype(BF)
    w6[level] = s6[...]
    for p, q in pillar:
        send(s6, w6.at[level], S_LEVEL, R_LEVEL, p, q)
    merge(0)
    for n in range(3):
        arrived(r2.at[n], R_SUM + n)

    for z in range(2):
        acc = s1[0, z].astype(F32)
        for m in range(3):
            acc = acc + r2[m, z].astype(F32)
        tiles = [
            acc[:, :, s * BLOCK : (s + 1) * BLOCK].reshape(PROJ, BLOCK).T for s in range(SLOTS)
        ]
        for k in range(QBLOCKS):
            val = jnp.zeros((BLOCK, PROJ), F32)
            for s in range(SLOTS):
                hit = (kb_ref[y, s] == k) & (s < len_ref[y])
                val = val + jnp.where(hit, tiles[s], 0.0)
            dense[z * QBLOCKS + k] = val.astype(BF)

    def share(g):
        at = pl.multiple_of(lax.rem(g, 2) * TILE_ROWS, TILE_ROWS)
        return dense.at[g // 2, pl.ds(at, TILE_ROWS), :]

    r4[me] = share(me)[...]
    for g, p, q in plane:
        send(share(g), r4.at[me], S_TILE, R_TILE, p, q)
    def turn_back(w):
        arrived(back_s.at[pl.ds(0, ROWS - 1)], R_PAIR + w)
        back_s[r * COL_WIDTH + w] = dpair_s[w, rows, :]

        @pl.loop(0, ROWS)
        def _(n):
            j = n * COL_WIDTH + w
            flat_s[pl.ds(j, TILE_ROWS, stride=TILE_COLS), :] = back_s[j].astype(F32)

    stay = []
    for w in range(3):
        turn_back(w)
    arrived(w6.at[pl.ds(0, PILLAR - 1)], R_LEVEL)
    tot = w6[0].astype(F32)
    for n in range(1, PILLAR):
        tot = tot + w6[n].astype(F32)
    wtot[...] = tot.astype(BF)
    stay.append(pltpu.make_async_copy(wtot, wsum_ref.at[myrows, :], local_sem.at[2]))
    stay[-1].start()
    for _, p, q in flat:
        send(wtot, wsum_ref.at[myrows, :], S_LAST, R_LAST, p, q)
    arrived(r4.at[pl.ds(0, PLANE - 1)], R_TILE)
    val = r4[0].astype(F32)
    for n in range(1, PLANE):
        val = val + r4[n].astype(F32)
    db_ref[...] = val.T
    turn_back(3)
    dp_ref[...] = flat_s[...].reshape(TILE_ROWS, TILE_COLS, PROJ).astype(BF)
    arrived(r5.at[pl.ds(0, PLANE - 1)], R_LAST)
    for cp in stay:
        cp.wait()
    for ref, n in (
        (r4.at[pl.ds(0, PLANE - 1)], S_BIAS),
        (actt.at[pl.ds(0, 28)], S_ACT),
        (gradt.at[pl.ds(0, 28)], S_GRAD),
        (mine, S_OWN),
        (r2, S_Y),
        (r2, S_FWD),
        (r1, S_SIB),
        (r2, S_SUM),
        (r4.at[pl.ds(0, PLANE - 1)], S_TILE),
        (back_s.at[pl.ds(0, 28)], S_PAIR),
        (r5.at[pl.ds(0, PLANE - 1)], S_PART),
        (w6.at[pl.ds(0, PILLAR - 1)], S_LEVEL),
        (r5.at[pl.ds(0, PLANE - 1)], S_LAST),
    ):
        settle(ref, send_sem.at[n])


def fused(key_blocks, list_len, act, grad, bias, *weights):
    any_ = pl.BlockSpec(memory_space=pl.ANY)
    smem = pl.BlockSpec(memory_space=pltpu.SMEM)
    vmem = pl.BlockSpec(memory_space=pltpu.VMEM)
    dma = pltpu.SemaphoreType.DMA
    flip = (TILE_COLS, TILE_ROWS, PROJ)
    cols = (COL_WIDTH, TOKENS, PROJ)
    tiles = (COL_WIDTH, QBLOCKS, PROJ, BLOCK)
    slots = (COL_WIDTH, QBLOCKS, SLOTS, PROJ, BLOCK)
    whole = (QBLOCKS, HEADS, BLOCK, WIDE)
    piece = (HEADS, TILE_COLS, WIDE)
    return pl.pallas_call(
        fused_kernel,
        out_shape=(
            jax.ShapeDtypeStruct((TILE_ROWS, TILE_COLS, PROJ), BF),
            jax.ShapeDtypeStruct((PROJ, TILE_ROWS), F32),
            jax.ShapeDtypeStruct((WPAD, PROJ), BF),
        ),
        in_specs=[smem] * 2 + [any_] * 2 + [vmem] * 6,
        out_specs=(vmem, vmem, any_),
        scratch_shapes=[
            pltpu.VMEM((TILE_ROWS * TILE_COLS, PROJ), F32),
            pltpu.VMEM(flip, BF), pltpu.VMEM(flip, BF),
            pltpu.VMEM(cols, BF), pltpu.VMEM(cols, BF),
            pltpu.VMEM((TILE_ROWS, PROJ), BF), pltpu.VMEM((ROWS, TILE_ROWS, PROJ), BF),
            pltpu.VMEM((ROWS, TILE_ROWS, PROJ), BF), pltpu.VMEM((2, *piece), BF), pltpu.VMEM(whole, BF),
            pltpu.VMEM((4 * PROJ, PROJ), BF),
            pltpu.VMEM((COL_WIDTH, QBLOCKS, PROJ, HEADS * BLOCK), BF),
            pltpu.VMEM((COL_WIDTH, QBLOCKS, HEADS * BLOCK, PROJ), BF),
            pltpu.VMEM(tiles, BF), pltpu.VMEM(tiles, BF),
            pltpu.VMEM(tiles, BF), pltpu.VMEM(tiles, BF),
            pltpu.VMEM(tiles, F32), pltpu.VMEM(tiles, F32),
            pltpu.VMEM(tiles, BF), pltpu.VMEM(tiles, BF), pltpu.VMEM(tiles, BF),
            pltpu.VMEM(slots, F32), pltpu.VMEM(slots, F32),
            pltpu.VMEM((QBLOCKS, WIDE, HEADS * BLOCK), F32),
            pltpu.VMEM((QBLOCKS, WIDE, HEADS * BLOCK), F32),
            pltpu.VMEM((2 * PROJ, PROJ), F32), pltpu.VMEM((PROJ, 2 * PROJ), F32),
            pltpu.VMEM((PROJ, PROJ), F32), pltpu.VMEM((COL_WIDTH, PROJ, TOKENS), BF),
            pltpu.VMEM((COL_WIDTH, 2 * PROJ, TOKENS), BF),
            pltpu.VMEM((COL_WIDTH, TOKENS, 2 * PROJ), BF), pltpu.VMEM(cols, BF),
            pltpu.VMEM((2, TILE_ROWS, TILE_COLS, PROJ), BF), pltpu.VMEM(flip, BF),
            pltpu.VMEM((WPART, PROJ), BF), dma((3,)),
            pltpu.VMEM(whole, BF), pltpu.VMEM((QBLOCKS, 2, *piece), BF),
            pltpu.VMEM((QBLOCKS, 2, *piece), BF), pltpu.VMEM((3, 2, *piece), BF),
            pltpu.VMEM((2 * QBLOCKS, BLOCK, PROJ), BF), pltpu.VMEM((PLANE, TILE_ROWS, PROJ), BF),
            pltpu.VMEM((WPAD, PROJ), BF), pltpu.VMEM((PLANE, WPART, PROJ), BF),
            pltpu.VMEM((WPART, PROJ), BF), pltpu.VMEM((PILLAR, WPART, PROJ), BF),
            dma((N_SEND,)), dma((N_RECV,)),
        ],
        compiler_params=pltpu.CompilerParams(
            collective_id=0, has_side_effects=True, vmem_limit_bytes=60 * 1024 * 1024
        ),
        name="attend_back",
    )(key_blocks, list_len, act, grad, bias, *weights)


CHUNKS = 4


def finish_kernel(dp_ref, db_ref, ws_ref, *refs):
    pair_ref, bias_ref, w_refs = refs[0], refs[1], refs[2:7]
    pair_s, bias_s, ws_s, w_s, get, put = refs[7:]
    size = TILE_ROWS // CHUNKS
    cuts = [pl.ds(n * size, size) for n in range(CHUNKS)]
    moves = [(ws_ref, ws_s), (db_ref, bias_s)]
    moves += [(dp_ref.at[cut], pair_s.at[cut]) for cut in cuts]
    loads = [pltpu.make_async_copy(a, b, get.at[n]) for n, (a, b) in enumerate(moves)]
    for cp in loads:
        cp.start()
    outs = [(bias_s, bias_ref)] + [(pair_s.at[cut], pair_ref.at[cut]) for cut in cuts]
    outs += [(w_s.at[n], ref) for n, ref in enumerate(w_refs)]
    stores = [pltpu.make_async_copy(a, b, put.at[n]) for n, (a, b) in enumerate(outs)]
    for n in range(1 + CHUNKS):
        loads[1 + n].wait()
        stores[n].start()
    loads[0].wait()
    for n in range(5):
        w_s[n] = ws_s[n * PROJ : (n + 1) * PROJ, :].astype(F32)
        stores[1 + CHUNKS + n].start()
    for cp in stores:
        cp.wait()


def finish(dp, db, ws):
    any_ = pl.BlockSpec(memory_space=pl.ANY)
    dma = pltpu.SemaphoreType.DMA
    return pl.pallas_call(
        finish_kernel,
        out_shape=(
            jax.ShapeDtypeStruct(dp.shape, BF),
            jax.ShapeDtypeStruct(db.shape, F32),
        )
        + (jax.ShapeDtypeStruct((PROJ, PROJ), F32),) * 5,
        in_specs=[any_] * 3,
        out_specs=(any_,) * 7,
        scratch_shapes=[
            pltpu.VMEM(dp.shape, BF), pltpu.VMEM(db.shape, F32), pltpu.VMEM(ws.shape, BF),
            pltpu.VMEM((5, PROJ, PROJ), F32), dma((2 + CHUNKS,)), dma((6 + CHUNKS,)),
        ],
        compiler_params=pltpu.CompilerParams(vmem_limit_bytes=60 * 1024 * 1024),
        name="finish",
    )(dp, db, ws)


def on_device(
    pair_act, out_grad, tri_bias, w_query, w_key, w_value, w_gate, w_out, key_blocks, list_len
):
    bias = jnp.transpose(tri_bias, (0, 2, 1)).reshape(PROJ, TILE_ROWS)
    d_pair, db, *d_w = finish(
        *fused(
            key_blocks, list_len, pair_act, out_grad, bias, w_query, w_key, w_value, w_gate, w_out
        )
    )
    d_bias = jnp.transpose(db.reshape(HEADS, TILE_COLS, TILE_ROWS), (0, 2, 1))
    return (d_pair, d_bias, *d_w)


def solution(mesh):
    in_specs = (
        P("row", "col", None), P("row", "col", None), P(None, "row", "col"),
        P(), P(), P(), P(), P(), P(), P(),
    )
    out_specs = (P("row", "col", None), P(None, "row", "col"), P(), P(), P(), P(), P())
    return jax.shard_map(
        on_device, mesh=mesh, in_specs=in_specs, out_specs=out_specs, check_vma=False
    )
```
